512 devices in a mesh: gx: 32 (over y, x), gy: 16 (over z, core).
Axes of the slice: x: 4, y: 8, z: 8, core: 2. Of those that a mesh axis runs over, the one named last changes fastest.
Arguments:
- gradient: float32 [19, 64, 128, 128], P(None, 'gx', 'gy'), may hold values from -60 to 60
- steady_state: float32 [19, 64, 128, 128], P(None, 'gx', 'gy'), may hold values from 0.02 to 0.4
- enter_weight: float32 [128, 19], replicated, may hold values from -12 to 12
- middle_weight: float32 [128, 128], replicated, may hold values from -1.08 to 1.08
- leave_weight: float32 [19, 128], replicated, may hold values from -0.036 to 0.036
- links: int32 [2, 64, 128, 128], P(None, 'gx', 'gy'), may hold values from 0 to 1023, as said below
Outputs:
- adjoint: float32 [19, 64, 128, 128], P(None, 'gx', 'gy')
The draws below stay inside these ranges and needn't reach their ends.
Inputs may be any that keep to these rules, and one draw needn't show every extreme that they name: Bit k of links is 1 exactly when the cell at offset c_k is solid or lies outside the lattice; about one cell in eight is solid, and one block of 3 x 3 x 3 cells is solid, so some cell has every bit set in both words.
All inputs are finite; a program needn't handle non-finite values.
Results may differ from the reference program's by a relative error of at most 0.0003.
Values sent between devices are 32-bit elements; how exact they have to be, the bound alone decides.
No kernel may reach another device: no remote copies, remote signals or barrier semaphores. Data moves between devices by JAX's collectives and lax.ppermute only.
A program may use at most 64 MiB of HBM per device.

```python
import math
import jax
import jax.numpy as jnp
from jax import lax

Q = 19
HID = 128
ITERS = 3
NZ = 128
NX = 64
NY = 128


velocities = ((1, 0, 0), (-1, 0, 0), (0, 1, 0), (0, -1, 0), (1, 1, 0), (-1, -1, 0), (1, -1, 0), (-1, 1, 0), (1, 0, 1), (-1, 0, -1), (1, 0, -1), (-1, 0, 1), (0, 1, 1), (0, -1, -1), (0, 1, -1), (0, -1, 1), (0, 0, 1), (0, 0, -1), (0, 0, 0))


def draw_gradient(key, part):
    first, second = jax.random.split(key, 2)
    scales = jnp.exp(jnp.log(10.0) * (jax.random.uniform(first, (Q, 1, 1, 1), dtype=jnp.float32) - 0.5))
    across = 1.0 + 2.0 * jnp.arange(NX, dtype=jnp.float32).reshape(1, NX, 1, 1) / max(NX - 1, 1)
    noise = jnp.clip(jax.random.normal(second, (Q, NX, NY, NZ), dtype=jnp.float32), -6.0, 6.0)
    return (noise * scales * across).astype(jnp.float32)


def draw_links(key, part):
    solid = (jax.random.randint(jax.random.fold_in(key, 11), (NX, NY, NZ), 0, 8) == 0).astype(jnp.int32)
    centre_x = jax.random.randint(jax.random.fold_in(key, 21), (), 1, NX - 1)
    centre_y = jax.random.randint(jax.random.fold_in(key, 22), (), 1, NY - 1)
    centre_z = jax.random.randint(jax.random.fold_in(key, 23), (), 1, NZ - 1)
    near_x = (jnp.abs(jnp.arange(NX, dtype=jnp.int32) - centre_x) <= 1).astype(jnp.int32).reshape(NX, 1, 1)
    near_y = (jnp.abs(jnp.arange(NY, dtype=jnp.int32) - centre_y) <= 1).astype(jnp.int32).reshape(1, NY, 1)
    near_z = (jnp.abs(jnp.arange(NZ, dtype=jnp.int32) - centre_z) <= 1).astype(jnp.int32).reshape(1, 1, NZ)
    solid = jnp.maximum(solid, near_x * near_y * near_z)
    padded = jnp.pad(solid, 1, constant_values=1)
    low_word = jnp.zeros((NX, NY, NZ), jnp.int32)
    high_word = jnp.zeros((NX, NY, NZ), jnp.int32)
    for member, (step_x, step_y, step_z) in enumerate(velocities):
        piece = padded[1 + step_x:1 + step_x + NX, 1 + step_y:1 + step_y + NY, 1 + step_z:1 + step_z + NZ]
        if member < 10:
            low_word = low_word + piece * 2 ** member
        else:
            high_word = high_word + piece * 2 ** (member - 10)
    return jnp.stack([low_word, high_word])


def levels(rng, extent, cuts, low, largest):
    def one(dim, blocks):
        steps = jax.random.uniform(jax.random.fold_in(jax.random.fold_in(rng, 6), dim), (blocks,), jnp.float32, low / len(cuts), largest / len(cuts))
        return jnp.repeat(jnp.exp(steps), extent[dim] // blocks).reshape((-1,) + (1,) * (len(extent) - dim - 1))

    loudness = one(*cuts[0])
    for cut in cuts[1:]:
        loudness = loudness * one(*cut)
    return loudness


def gaussian(rng, extent, scale, bound, kind=jnp.bfloat16):
    values = scale * jax.random.normal(rng, extent, jnp.float32)
    return jnp.clip(values, min=-bound, max=bound).astype(kind)


def setup_inputs(seed: int = 0) -> dict:
    keys = jax.random.split(jax.random.key(seed), 7)
    gradient = draw_gradient(jax.random.fold_in(keys[6], 71), 0)
    steady_state = jnp.clip(jnp.exp(math.log(0.4) - 2.9957323 * jax.random.uniform(keys[1], (Q, NX, NY, NZ), jnp.float32) ** levels(keys[1], (Q, NX, NY, NZ), ((1, 32), (2, 16)), -0.2, 0.2)), 0.02, 0.4)
    enter_weight = gaussian(keys[2], (HID, Q), 2.0, 12.0, jnp.float32)
    middle_weight = gaussian(keys[3], (HID, HID), 0.18, 1.08, jnp.float32)
    leave_weight = gaussian(keys[4], (Q, HID), 0.006, 0.036, jnp.float32)
    links = draw_links(jax.random.fold_in(keys[6], 71), 0)
    return {"gradient": gradient, "steady_state": steady_state, "enter_weight": enter_weight, "middle_weight": middle_weight, "leave_weight": leave_weight, "links": links}


velocities = ((1, 0, 0), (-1, 0, 0), (0, 1, 0), (0, -1, 0), (1, 1, 0), (-1, -1, 0), (1, -1, 0), (-1, 1, 0), (1, 0, 1), (-1, 0, -1), (1, 0, -1), (-1, 0, 1), (0, 1, 1), (0, -1, -1), (0, 1, -1), (0, -1, 1), (0, 0, 1), (0, 0, -1), (0, 0, 0))
retained = 0.5

def shift_depth(plane, step_z):
    if step_z == 1:
        return jnp.concatenate([plane[..., 1:], jnp.zeros_like(plane[..., :1])], axis=-1)
    if step_z == -1:
        return jnp.concatenate([jnp.zeros_like(plane[..., :1]), plane[..., :-1]], axis=-1)
    return plane

def swap_pairs(field):
    moving = field[:Q - 1]
    flipped = moving.reshape((9, 2) + moving.shape[1:])[:, ::-1].reshape(moving.shape)
    return jnp.concatenate([flipped, field[Q - 1:]], axis=0)

def open_links(links):
    return jnp.stack([(1 - links[member // 10] // 2 ** (member % 10) % 2).astype(jnp.float32) for member in range(Q)])

def pull_planes(field, padded):
    size_x = field.shape[1]
    size_y = field.shape[2]
    planes = []
    for member, (step_x, step_y, step_z) in enumerate(velocities):
        if step_x != 0 or step_y != 0:
            plane = padded[member, 1 + step_x:1 + step_x + size_x, 1 + step_y:1 + step_y + size_y, :]
        else:
            plane = field[member]
        planes.append(shift_depth(plane, step_z))
    return jnp.stack(planes)

def slopes(state_flat, enter_weight, middle_weight):
    hidden_one = jnp.tanh(jnp.dot(enter_weight, state_flat, precision=lax.Precision.HIGHEST, preferred_element_type=jnp.float32))
    hidden_two = jnp.tanh(jnp.dot(middle_weight, hidden_one, precision=lax.Precision.HIGHEST, preferred_element_type=jnp.float32))
    return (1.0 - hidden_one * hidden_one, 1.0 - hidden_two * hidden_two)

def collide_back(flat, slope_one, slope_two, enter_weight, middle_weight, leave_weight):
    carried = jnp.dot(leave_weight.T, flat, precision=lax.Precision.HIGHEST, preferred_element_type=jnp.float32) * slope_two
    carried = jnp.dot(middle_weight.T, carried, precision=lax.Precision.HIGHEST, preferred_element_type=jnp.float32) * slope_one
    return retained * flat + jnp.dot(enter_weight.T, carried, precision=lax.Precision.HIGHEST, preferred_element_type=jnp.float32)

def least_squares(hess, beta):
    rows = [list(line) for line in hess]
    target = [beta] + [beta * 0.0 for column in range(ITERS)]
    for column in range(ITERS):
        upper = rows[column][column]
        lower = rows[column + 1][column]
        radius = jnp.sqrt(upper * upper + lower * lower)
        cosine = upper / radius
        sine = lower / radius
        for other in range(column, ITERS):
            first_value = rows[column][other]
            second_value = rows[column + 1][other]
            rows[column][other] = cosine * first_value + sine * second_value
            rows[column + 1][other] = cosine * second_value - sine * first_value
        first_value = target[column]
        second_value = target[column + 1]
        target[column] = cosine * first_value + sine * second_value
        target[column + 1] = cosine * second_value - sine * first_value
    coeffs = [None] * ITERS
    for column in reversed(range(ITERS)):
        accum = target[column]
        for other in range(column + 1, ITERS):
            accum = accum - rows[column][other] * coeffs[other]
        coeffs[column] = accum / rows[column][column]
    return coeffs

def reference(gradient, steady_state, enter_weight, middle_weight, leave_weight, links):
    opened = open_links(links)
    state_planes = jnp.moveaxis(steady_state, 1, 0)

    def apply_operator(field):
        padded = jnp.pad(field, ((0, 0), (1, 1), (1, 1), (0, 0)))
        pulled = pull_planes(field, padded)
        read = opened[Q - 1] * (opened * pulled + (1.0 - opened) * swap_pairs(field))

        def per_plane(pair):
            plane, state = pair
            slope_one, slope_two = slopes(state.reshape(Q, -1), enter_weight, middle_weight)
            result = collide_back(plane.reshape(Q, -1), slope_one, slope_two, enter_weight, middle_weight, leave_weight)
            return result.reshape(plane.shape)
        collided = lax.map(per_plane, (jnp.moveaxis(read, 1, 0), state_planes))
        return field - jnp.moveaxis(collided, 0, 1)
    beta = jnp.sqrt(jnp.sum(gradient * gradient))
    basis = [gradient / beta]
    hess = [[beta * 0.0 for column in range(ITERS)] for line in range(ITERS + 1)]
    for column in range(ITERS):
        image = apply_operator(basis[column])
        for row_at in range(column + 1):
            hess[row_at][column] = jnp.sum(image * basis[row_at])
        for row_at in range(column + 1):
            image = image - hess[row_at][column] * basis[row_at]
        length = jnp.sqrt(jnp.sum(image * image))
        hess[column + 1][column] = length
        if column + 1 < ITERS:
            basis.append(image / length)
    coeffs = least_squares(hess, beta)
    adjoint = coeffs[0] * basis[0]
    for column in range(1, ITERS):
        adjoint = adjoint + coeffs[column] * basis[column]
    return adjoint
```

```python
import jax
import jax.numpy as jnp
from jax import lax
from jax.experimental import pallas as pl
from jax.experimental.pallas import tpu as pltpu
from jax.sharding import PartitionSpec as P

Q = 19
HID = 128
ITERS = 3
ROWS = 24
SHRINK = 16.0
FLOOR = 1e-10

ORDER = (0, 4, 6, 8, 10, 2, 12, 14, 1, 5, 7, 9, 11, 3, 13, 15, 16, 17, 18)

F32 = jnp.float32
BF16 = jnp.bfloat16
VM = pl.BlockSpec(memory_space=pltpu.VMEM)


def call(kernel, outs, *args):
    return pl.pallas_call(
        kernel,
        out_shape=[jax.ShapeDtypeStruct(shape, kind) for shape, kind in outs],
        in_specs=[VM] * len(args),
        out_specs=[VM] * len(outs),
    )(*args)


def high(x):
    return x.astype(BF16).astype(F32)


def rows_dot(weights, x):
    top = high(x)
    stack = jnp.concatenate([top, top, x - top, jnp.zeros((8, x.shape[1]), F32)], axis=0)
    return jnp.dot(weights, stack.astype(BF16), preferred_element_type=F32)


def wide_dot(weights, x):
    top = x.astype(BF16)
    rest = (x - top.astype(F32)).astype(BF16)
    both = jnp.dot(weights, jnp.concatenate([top, rest], axis=0), preferred_element_type=F32)
    half = weights.shape[0] // 2
    return both[:half] + both[half:]


def weights_kernel(enter_t, middle, leave, enter_rows, leave_rows, middle_wide, middle_t_wide, enter_t_wide):
    def ordered(ref):
        rows = [ref[k : k + 1, :] for k in ORDER]
        return jnp.concatenate(rows + [jnp.zeros((ROWS - Q, HID), F32)], axis=0)

    def tall(rows):
        top = high(rows)
        stack = jnp.concatenate([top, rows - top, top, jnp.zeros((HID - 3 * ROWS, HID), F32)], axis=0)
        return stack.T.astype(BF16)

    def wide(mat):
        top = high(mat)
        rest = mat - top
        upper = jnp.concatenate([top, top], axis=1)
        lower = jnp.concatenate([rest, jnp.zeros_like(rest)], axis=1)
        return jnp.concatenate([upper, lower], axis=0).astype(BF16)

    enter = ordered(enter_t)
    enter_rows[...] = tall(enter)
    leave_rows[...] = tall(ordered(leave))
    middle_wide[...] = wide(middle[...])
    middle_t_wide[...] = wide(middle[...].T)
    scaled = enter * (1.0 / SHRINK)
    enter_t_wide[...] = wide(jnp.concatenate([scaled, jnp.zeros((8, HID), F32)], axis=0))


def prepare_kernel(sx, sy, gradient, steady, links, field, state, to_low, to_high):
    blank = jnp.zeros((8, 128), F32)
    for x in range(sx):
        for y in range(sy):
            at = (x * sy + y) * ROWS + 16
            field[pl.ds(at, 8), :] = blank
            state[pl.ds(at, 8), :] = blank
    for x in range(sx):
        for row, k in enumerate(ORDER):
            field[pl.ds(x * sy * ROWS + row, sy, stride=ROWS), :] = gradient[k, x]
            state[pl.ds(x * sy * ROWS + row, sy, stride=ROWS), :] = steady[k, x]
        for word in range(2):
            state[pl.ds(x * sy * ROWS + Q + word, sy, stride=ROWS), :] = links[word, x].astype(F32)
    at = 0
    for ref, depth in ((field, 3), (state, 2)):
        for x in range(sx):
            size = depth * ROWS
            to_low[pl.ds(at, size), :] = ref[pl.ds(x * sy * ROWS, size), :]
            to_high[pl.ds(at, size), :] = ref[pl.ds((x * sy + sy - depth) * ROWS, size), :]
            at += size


def sublane():
    return lax.broadcasted_iota(jnp.int32, (8, 128), 0)


def row_constants(values):
    row = sublane()
    out = jnp.zeros((8, 128), jnp.int32)
    for at, value in enumerate(values):
        out = jnp.where(row == at, value, out)
    return out


def codes_of(tail):
    word_0 = jnp.broadcast_to(tail[3:4, :].astype(jnp.int32), (8, 128))
    word_1 = jnp.broadcast_to(tail[4:5, :].astype(jnp.int32), (8, 128))
    solid = (word_1 & (1 << (18 - 10))) != 0
    codes = []
    for group in range(3):
        members = [ORDER[group * 8 + i] if group * 8 + i < Q else -1 for i in range(8)]
        second = row_constants([1 if k >= 10 else 0 for k in members])
        bit = row_constants([0 if k < 0 else 1 << (k % 10) for k in members])
        pad = row_constants([1 if k < 0 else 0 for k in members])
        word = jnp.where(second == 1, word_1, word_0)
        code = jnp.where((word & bit) != 0, 1.0, 0.0)
        codes.append(jnp.where(jnp.logical_or(solid, pad == 1), 2.0, code))
    return codes


def slopes_of(columns, enter_rows, middle_wide, slope_one, slope_two, codes):
    enter = enter_rows[:, 0:80]
    middle = middle_wide[...]
    for at in range(0, len(columns), 2):
        pair = [ref[pl.ds(offset, ROWS), :] for ref, offset in columns[at : at + 2]]
        hidden = jnp.tanh(rows_dot(enter, jnp.concatenate(pair, axis=1)))
        one = 1.0 - hidden * hidden
        hidden = jnp.tanh(wide_dot(middle, hidden))
        two = 1.0 - hidden * hidden
        for i in range(2):
            slope_one[at + i] = one[:, i * 128 : (i + 1) * 128]
            slope_two[at + i] = two[:, i * 128 : (i + 1) * 128]
            for group, code in enumerate(codes_of(pair[i][16:24, :])):
                codes[at + i, group * 8 : group * 8 + 8, :] = code


def own_slopes_kernel(count, state, enter_rows, middle_wide, slope_one, slope_two, codes):
    columns = [(state, i * ROWS) for i in range(count)]
    slopes_of(columns, enter_rows, middle_wide, slope_one, slope_two, codes)


def halo_slopes_kernel(sx, low, high_, enter_rows, middle_wide, slope_one, slope_two, codes):
    columns = []
    for x in range(sx):
        for ref in (low, high_):
            for row in range(2):
                columns.append((ref, (sx * 3 + x * 2 + row) * ROWS))
    slopes_of(columns, enter_rows, middle_wide, slope_one, slope_two, codes)


def faces_kernel(sx, sy, field, low, high_, to_low, to_high):
    for row in range(-3, sy + 3):
        for x, group, out in ((0, 0, to_low), (sx - 1, 8, to_high)):
            out[row + 3] = column(sx, sy, field, low, high_, x, row, group)


def column(sx, sy, field, low, high_, x, row, group):
    if row < 0:
        return low[pl.ds((x * 3 + row + 3) * ROWS + group, 8), :]
    if row >= sy:
        return high_[pl.ds((x * 3 + row - sy) * ROWS + group, 8), :]
    return field[pl.ds((x * sy + row) * ROWS + group, 8), :]


def pull_column(get, code, x, row):
    at = sublane()
    straight = jnp.logical_or(at == 0, jnp.logical_or(at == 3, at == 4))
    first = jnp.logical_or(at == 3, at == 6)
    second = jnp.logical_or(at == 4, at == 7)
    own = [get(x, row, group) for group in (0, 8, 16)]
    out = []
    for group, step in ((0, 1), (8, -1)):
        value = jnp.where(straight, get(x + step, row, group), get(x, row + step, group))
        value = jnp.where(at == 1, get(x + step, row + step, group), value)
        value = jnp.where(at == 2, get(x + step, row - step, group), value)
        up = pltpu.roll(value, 127, 1)
        down = pltpu.roll(value, 1, 1)
        if step < 0:
            up, down = down, up
        out.append(jnp.where(first, up, jnp.where(second, down, value)))
    up = pltpu.roll(own[2], 127, 1)
    down = pltpu.roll(own[2], 1, 1)
    out.append(jnp.where(at == 0, up, jnp.where(at == 1, down, own[2])))
    swapped = jnp.where(at == 0, pltpu.roll(own[2], 7, 0), jnp.where(at == 1, pltpu.roll(own[2], 1, 0), own[2]))
    result = []
    for pulled, back, flag in zip(out, (own[1], own[0], swapped), (code(0), code(8), code(16))):
        result.append(jnp.where(flag == 0.0, pulled, jnp.where(flag == 1.0, back, 0.0)))
    return jnp.concatenate(result, axis=0)


def apply_rows(sx, first, last, get, table, leave_rows, middle_t_wide, enter_t_wide, put):
    leave = leave_rows[:, 0:80]
    middle = middle_t_wide[...]
    enter = enter_t_wide[...]
    for x in range(sx):
        for row in range(first, last, 2):
            reads, ones, twos = [], [], []
            for r in (row, row + 1):
                one, two, codes, at = table(x, r)
                reads.append(pull_column(get, lambda g: codes[at, g : g + 8, :], x, r))
                ones.append(one[at])
                twos.append(two[at])
            read = jnp.concatenate(reads, axis=1)
            carried = rows_dot(leave, read) * jnp.concatenate(twos, axis=1)
            carried = wide_dot(middle, carried) * jnp.concatenate(ones, axis=1)
            image = (0.5 / SHRINK) * read + wide_dot(enter, carried)[:ROWS]
            for i in range(2):
                put(x, row + i, image[:, i * 128 : (i + 1) * 128])


def table_of(sy, refs):
    one, two, codes, one_h, two_h, codes_h = refs

    def table(x, row):
        if 0 <= row < sy:
            return one, two, codes, x * sy + row
        return one_h, two_h, codes_h, x * 4 + (row + 2 if row < 0 else row - sy + 2)

    return table


def apply_kernel(sx, sy, step, *refs):
    if step == 1:
        field, low, high_ = refs[:3]
        refs = refs[3:]

        def inner(x, row, group):
            return column(sx, sy, field, low, high_, x, row, group)

    else:
        previous = refs[0]
        refs = refs[1:]
        depth = 4 - step
        height = sy + 2 * depth

        def inner(x, row, group):
            return previous[pl.ds((x * height + row + depth) * ROWS + group, 8), :]

    from_low, from_high = refs[:2]
    table = table_of(sy, refs[2:8])
    leave_rows, middle_t_wide, enter_t_wide = refs[8:11]
    refs = refs[11:]
    before = 4 - step

    def get(x, row, group):
        if x < 0:
            return from_low[row + before]
        if x >= sx:
            return from_high[row + before]
        return inner(x, row, group)

    after = 3 - step
    height_out = sy + 2 * after
    if step < 3:
        image, to_low, to_high = refs

        def put(x, row, value):
            image[pl.ds((x * height_out + row + after) * ROWS, ROWS), :] = value
            if x == 0:
                to_low[row + after] = value[0:8]
            if x == sx - 1:
                to_high[row + after] = value[8:16]

        apply_rows(sx, -after, sy + after, get, table, leave_rows, middle_t_wide, enter_t_wide, put)
        return

    field, image_one, out = refs
    totals = [jnp.zeros((8, 128), F32) for _ in range(10)]

    def put(x, row, value):
        for group in (0, 8, 16):
            parts = (
                field[pl.ds((x * sy + row) * ROWS + group, 8), :],
                image_one[pl.ds((x * (sy + 4) + row + 2) * ROWS + group, 8), :],
                inner(x, row, group),
                value[group : group + 8],
            )
            at = 0
            for i in range(4):
                for j in range(i, 4):
                    totals[at] = totals[at] + parts[i] * parts[j]
                    at += 1

    apply_rows(sx, 0, sy, get, table, leave_rows, middle_t_wide, enter_t_wide, put)
    sums = jnp.concatenate(
        [jnp.sum(total, axis=0, keepdims=True) for total in totals] + [jnp.zeros((6, 128), F32)], axis=0
    )
    sums = jnp.broadcast_to(jnp.sum(sums, axis=1, keepdims=True), (16, 128))
    place = lax.broadcasted_iota(jnp.int32, (16, 128), 0) == lax.broadcasted_iota(jnp.int32, (16, 128), 1)
    line = jnp.sum(jnp.where(place, sums, 0.0), axis=0, keepdims=True)
    for i in range(out.shape[0]):
        out[i] = line


def least_squares(hess, target):
    rows = [list(line) for line in hess]
    target = list(target)
    for col in range(ITERS):
        upper = rows[col][col]
        lower = rows[col + 1][col]
        radius = jnp.sqrt(upper * upper + lower * lower)
        cosine = upper / radius
        sine = lower / radius
        for other in range(col, ITERS):
            first_value = rows[col][other]
            second_value = rows[col + 1][other]
            rows[col][other] = cosine * first_value + sine * second_value
            rows[col + 1][other] = cosine * second_value - sine * first_value
        first_value = target[col]
        second_value = target[col + 1]
        target[col] = cosine * first_value + sine * second_value
        target[col + 1] = cosine * second_value - sine * first_value
    coeffs = [None] * ITERS
    for col in reversed(range(ITERS)):
        accum = target[col]
        for other in range(col + 1, ITERS):
            accum = accum - rows[col][other] * coeffs[other]
        coeffs[col] = accum / rows[col][col]
    return coeffs


def finish_kernel(sx, sy, parts, gradient, image_one, image_two, out):
    total = parts[0]
    for i in range(1, parts.shape[0]):
        total = total + parts[i]
    total = jnp.broadcast_to(total, (8, 128))
    lane = lax.broadcasted_iota(jnp.int32, (8, 128), 1)
    gram = [[None] * 4 for _ in range(4)]
    at = 0
    for i in range(4):
        for j in range(i, 4):
            one = jnp.sum(jnp.where(lane == at, total, 0.0), axis=1, keepdims=True)
            gram[i][j] = gram[j][i] = jnp.broadcast_to(one, (8, 128))
            at += 1
    size = [jnp.sqrt(gram[i][i]) for i in range(4)]
    inverse = [1.0 / value for value in size]
    cosines = [[gram[i][j] * inverse[i] * inverse[j] for j in range(4)] for i in range(4)]
    zero = jnp.zeros((8, 128), F32)
    one = zero + 1.0
    lower = [[zero] * 4 for _ in range(4)]
    for i in range(4):
        for j in range(i + 1):
            value = one if i == j else cosines[i][j]
            for k in range(j):
                value = value - lower[i][k] * lower[j][k]
            lower[i][j] = jnp.sqrt(jnp.maximum(value, FLOOR)) if i == j else value / lower[j][j]
    hess = [[zero] * ITERS for _ in range(ITERS + 1)]
    for j in range(ITERS):
        ratio = SHRINK * size[j + 1] * inverse[j]
        for i in range(j + 2):
            hess[i][j] = lower[j][i] - ratio * lower[j + 1][i]
    coeffs = least_squares(hess, [one, zero, zero, zero])
    scaled = [coeffs[j] * size[0] * inverse[j] for j in range(ITERS)]
    for x in range(sx):
        for row, k in enumerate(ORDER):
            second = image_one[pl.ds((x * (sy + 4) + 2) * ROWS + row, sy, stride=ROWS), :]
            third = image_two[pl.ds((x * (sy + 2) + 1) * ROWS + row, sy, stride=ROWS), :]
            out[k, x] = scaled[0] * gradient[k, x] + scaled[1] * second + scaled[2] * third


def exchange(axis, to_low, to_high):
    count = lax.axis_size(axis)
    forward = [(i, i + 1) for i in range(count - 1)]
    backward = [(i + 1, i) for i in range(count - 1)]
    return lax.ppermute(to_high, axis, forward), lax.ppermute(to_low, axis, backward)


def per_device(gradient, steady_state, enter_weight, middle_weight, leave_weight, links):
    sx, sy, sz = gradient.shape[1:]
    own = sx * sy

    def bind(kernel, *static):
        def bound(*refs):
            kernel(*static, *refs)

        bound.__name__ = kernel.__name__
        return bound

    flat = (own * ROWS, sz)
    message = (sx * 5 * ROWS, sz)
    field, state, to_low, to_high = call(
        bind(prepare_kernel, sx, sy),
        [(flat, F32), (flat, F32), (message, F32), (message, F32)],
        gradient, steady_state, links,
    )
    low, high_ = exchange("gy", to_low, to_high)
    enter_rows, leave_rows, middle_wide, middle_t_wide, enter_t_wide = call(
        weights_kernel,
        [((HID, HID), BF16), ((HID, HID), BF16), ((2 * HID, 2 * HID), BF16), ((2 * HID, 2 * HID), BF16), ((64, 2 * HID), BF16)],
        enter_weight.T, middle_weight, leave_weight,
    )

    def tables(count):
        return [((count, HID, sz), F32), ((count, HID, sz), F32), ((count, ROWS, sz), F32)]

    own_table = call(bind(own_slopes_kernel, own), tables(own), state, enter_rows, middle_wide)
    to_low, to_high = call(
        bind(faces_kernel, sx, sy), [((sy + 6, 8, sz), F32)] * 2, field, low, high_
    )
    from_low, from_high = exchange("gx", to_low, to_high)
    halo_table = call(
        bind(halo_slopes_kernel, sx), tables(sx * 4), low, high_, enter_rows, middle_wide
    )
    shared = (*own_table, *halo_table, leave_rows, middle_t_wide, enter_t_wide)

    def image_shapes(depth):
        height = sy + 2 * depth
        return [((sx * height * ROWS, sz), F32), ((height, 8, sz), F32), ((height, 8, sz), F32)]

    image_one, to_low, to_high = call(
        bind(apply_kernel, sx, sy, 1), image_shapes(2), field, low, high_, from_low, from_high, *shared
    )
    from_low, from_high = exchange("gx", to_low, to_high)
    image_two, to_low, to_high = call(
        bind(apply_kernel, sx, sy, 2), image_shapes(1), image_one, from_low, from_high, *shared
    )
    from_low, from_high = exchange("gx", to_low, to_high)
    count_y = lax.axis_size("gy")
    count_x = lax.axis_size("gx")

    def last_kernel(*refs):
        *refs, field, image_one, out = refs
        apply_kernel(sx, sy, 3, *refs, field, image_one, out)

    (line,) = call(
        last_kernel, [((count_y, 1, sz), F32)], image_two, from_low, from_high, *shared, field, image_one
    )
    line = jnp.sum(lax.all_to_all(line, "gy", 0, 0), axis=0, keepdims=True)
    parts = lax.all_to_all(jnp.broadcast_to(line, (count_x, 1, sz)), "gx", 0, 0)
    (adjoint,) = call(
        bind(finish_kernel, sx, sy), [(gradient.shape, F32)], parts, gradient, image_one, image_two
    )
    return adjoint


def solution(mesh):
    in_specs = (
        P(None, "gx", "gy", None),
        P(None, "gx", "gy", None),
        P(),
        P(),
        P(),
        P(None, "gx", "gy", None),
    )
    out_specs = P(None, "gx", "gy", None)
    return jax.shard_map(
        per_device, mesh=mesh, in_specs=in_specs, out_specs=out_specs, check_vma=False
    )
```

```python
import jax
import jax.numpy as jnp
from jax import lax
from jax.experimental import pallas as pl
from jax.experimental.pallas import tpu as pltpu
from jax.sharding import PartitionSpec as P

Q = 19
HID = 128
ITERS = 3
ROWS = 24
SHRINK = 16.0
FLOOR = 1e-10
VMEM_BYTES = 16 * 1024 * 1024

ORDER = (0, 4, 6, 8, 10, 2, 12, 14, 1, 5, 7, 9, 11, 3, 13, 15, 16, 17, 18)

F32 = jnp.float32
BF16 = jnp.bfloat16
VM = pl.BlockSpec(memory_space=pltpu.VMEM)


def call(kernel, outs, *args):
    return pl.pallas_call(
        kernel,
        out_shape=[jax.ShapeDtypeStruct(shape, kind) for shape, kind in outs],
        in_specs=[VM] * len(args),
        out_specs=[VM] * len(outs),
        compiler_params=pltpu.CompilerParams(vmem_limit_bytes=VMEM_BYTES),
    )(*args)


def high(x):
    return x.astype(BF16).astype(F32)


def rows_dot(weights, x):
    top = high(x)
    stack = jnp.concatenate([top, top, x - top, jnp.zeros((8, x.shape[1]), F32)], axis=0)
    return jnp.dot(weights, stack.astype(BF16), preferred_element_type=F32)


def wide_dot(weights, x):
    top = x.astype(BF16)
    rest = (x - top.astype(F32)).astype(BF16)
    both = jnp.dot(weights, jnp.concatenate([top, rest], axis=0), preferred_element_type=F32)
    half = weights.shape[0] // 2
    return both[:half] + both[half:]


def staggered(chunks):
    waiting = list(chunks)
    running = []
    while waiting or running:
        if waiting:
            running.append(waiting.pop(0))
        for chunk in list(running):
            if next(chunk, None) is None:
                running.remove(chunk)


def weights_kernel(enter_t, middle, leave, enter_rows, leave_rows, middle_wide, middle_t_wide, enter_t_wide):
    def ordered(ref):
        rows = [ref[k : k + 1, :] for k in ORDER]
        return jnp.concatenate(rows + [jnp.zeros((ROWS - Q, HID), F32)], axis=0)

    def tall(rows):
        top = high(rows)
        stack = jnp.concatenate([top, rows - top, top, jnp.zeros((HID - 3 * ROWS, HID), F32)], axis=0)
        return stack.T.astype(BF16)

    def wide(mat):
        top = high(mat)
        rest = mat - top
        upper = jnp.concatenate([top, top], axis=1)
        lower = jnp.concatenate([rest, jnp.zeros_like(rest)], axis=1)
        return jnp.concatenate([upper, lower], axis=0).astype(BF16)

    enter = ordered(enter_t)
    enter_rows[...] = tall(enter)
    leave_rows[...] = tall(ordered(leave))
    middle_wide[...] = wide(middle[...])
    middle_t_wide[...] = wide(middle[...].T)
    scaled = enter * (1.0 / SHRINK)
    enter_t_wide[...] = wide(jnp.concatenate([scaled, jnp.zeros((8, HID), F32)], axis=0))


def prepare_kernel(sx, sy, gradient, steady, links, field, state, to_low, to_high):
    blank = jnp.zeros((8, 128), F32)
    for x in range(sx):
        for y in range(sy):
            at = (x * sy + y) * ROWS + 16
            field[pl.ds(at, 8), :] = blank
            state[pl.ds(at, 8), :] = blank
    for x in range(sx):
        for row, k in enumerate(ORDER):
            field[pl.ds(x * sy * ROWS + row, sy, stride=ROWS), :] = gradient[k, x]
            state[pl.ds(x * sy * ROWS + row, sy, stride=ROWS), :] = steady[k, x]
        for word in range(2):
            state[pl.ds(x * sy * ROWS + Q + word, sy, stride=ROWS), :] = links[word, x].astype(F32)
    at = 0
    for ref, depth in ((field, 3), (state, 2)):
        for x in range(sx):
            size = depth * ROWS
            to_low[pl.ds(at, size), :] = ref[pl.ds(x * sy * ROWS, size), :]
            to_high[pl.ds(at, size), :] = ref[pl.ds((x * sy + sy - depth) * ROWS, size), :]
            at += size


def sublane():
    return lax.broadcasted_iota(jnp.int32, (8, 128), 0)


def row_constants(values):
    row = sublane()
    out = jnp.zeros((8, 128), jnp.int32)
    for at, value in enumerate(values):
        out = jnp.where(row == at, value, out)
    return out


def codes_of(tail):
    word_0 = jnp.broadcast_to(tail[3:4, :].astype(jnp.int32), (8, 128))
    word_1 = jnp.broadcast_to(tail[4:5, :].astype(jnp.int32), (8, 128))
    solid = (word_1 & (1 << (18 - 10))) != 0
    codes = []
    for group in range(3):
        members = [ORDER[group * 8 + i] if group * 8 + i < Q else -1 for i in range(8)]
        second = row_constants([1 if k >= 10 else 0 for k in members])
        bit = row_constants([0 if k < 0 else 1 << (k % 10) for k in members])
        pad = row_constants([1 if k < 0 else 0 for k in members])
        word = jnp.where(second == 1, word_1, word_0)
        code = jnp.where((word & bit) != 0, 1.0, 0.0)
        codes.append(jnp.where(jnp.logical_or(solid, pad == 1), 2.0, code))
    return codes


def slopes_of(columns, enter_rows, middle_wide, slope_one, slope_two, codes):
    enter = enter_rows[:, 0:80]
    middle = middle_wide[...]

    def chunk(at):
        pair = [ref[pl.ds(offset, ROWS), :] for ref, offset in columns[at : at + 2]]
        hidden = jnp.tanh(rows_dot(enter, jnp.concatenate(pair, axis=1)))
        yield True
        one = 1.0 - hidden * hidden
        hidden = jnp.tanh(wide_dot(middle, hidden))
        yield True
        two = 1.0 - hidden * hidden
        for i in range(2):
            slope_one[at + i] = one[:, i * 128 : (i + 1) * 128]
            slope_two[at + i] = two[:, i * 128 : (i + 1) * 128]
            for group, code in enumerate(codes_of(pair[i][16:24, :])):
                codes[at + i, group * 8 : group * 8 + 8, :] = code

    staggered(chunk(at) for at in range(0, len(columns), 2))


def own_slopes_kernel(count, state, enter_rows, middle_wide, slope_one, slope_two, codes):
    columns = [(state, i * ROWS) for i in range(count)]
    slopes_of(columns, enter_rows, middle_wide, slope_one, slope_two, codes)


def halo_slopes_kernel(sx, low, high_, enter_rows, middle_wide, slope_one, slope_two, codes):
    columns = []
    for x in range(sx):
        for ref in (low, high_):
            for row in range(2):
                columns.append((ref, (sx * 3 + x * 2 + row) * ROWS))
    slopes_of(columns, enter_rows, middle_wide, slope_one, slope_two, codes)


def faces_kernel(sx, sy, field, low, high_, _, to_low, to_high):
    for row in range(-3, sy + 3):
        for x, group, out in ((0, 0, to_low), (sx - 1, 8, to_high)):
            out[row + 3] = column(sx, sy, field, low, high_, x, row, group)


def column(sx, sy, field, low, high_, x, row, group):
    if row < 0:
        return low[pl.ds((x * 3 + row + 3) * ROWS + group, 8), :]
    if row >= sy:
        return high_[pl.ds((x * 3 + row - sy) * ROWS + group, 8), :]
    return field[pl.ds((x * sy + row) * ROWS + group, 8), :]


def pull_column(get, code, x, row):
    at = sublane()
    straight = jnp.logical_or(at == 0, jnp.logical_or(at == 3, at == 4))
    first = jnp.logical_or(at == 3, at == 6)
    second = jnp.logical_or(at == 4, at == 7)
    own = [get(x, row, group) for group in (0, 8, 16)]
    out = []
    for group, step in ((0, 1), (8, -1)):
        value = jnp.where(straight, get(x + step, row, group), get(x, row + step, group))
        value = jnp.where(at == 1, get(x + step, row + step, group), value)
        value = jnp.where(at == 2, get(x + step, row - step, group), value)
        up = pltpu.roll(value, 127, 1)
        down = pltpu.roll(value, 1, 1)
        if step < 0:
            up, down = down, up
        out.append(jnp.where(first, up, jnp.where(second, down, value)))
    up = pltpu.roll(own[2], 127, 1)
    down = pltpu.roll(own[2], 1, 1)
    out.append(jnp.where(at == 0, up, jnp.where(at == 1, down, own[2])))
    swapped = jnp.where(at == 0, pltpu.roll(own[2], 7, 0), jnp.where(at == 1, pltpu.roll(own[2], 1, 0), own[2]))
    result = []
    for pulled, back, flag in zip(out, (own[1], own[0], swapped), (code(0), code(8), code(16))):
        result.append(jnp.where(flag == 0.0, pulled, jnp.where(flag == 1.0, back, 0.0)))
    return jnp.concatenate(result, axis=0)


def apply_rows(sx, first, last, get, table, leave_rows, middle_t_wide, enter_t_wide, put):
    leave = leave_rows[:, 0:80]
    middle = middle_t_wide[...]
    enter = enter_t_wide[...]

    def chunk(x, row):
        entries = [table(x, r) for r in (row, row + 1)]
        reads = [
            pull_column(get, lambda g, codes=codes, at=at: codes[at, g : g + 8, :], x, row + i)
            for i, (_, _, codes, at) in enumerate(entries)
        ]
        read = jnp.concatenate(reads, axis=1)
        yield True
        carried = rows_dot(leave, read) * jnp.concatenate([two[at] for _, two, _, at in entries], axis=1)
        yield True
        carried = wide_dot(middle, carried) * jnp.concatenate([one[at] for one, _, _, at in entries], axis=1)
        yield True
        image = (0.5 / SHRINK) * read + wide_dot(enter, carried)[:ROWS]
        for i in range(2):
            put(x, row + i, image[:, i * 128 : (i + 1) * 128])

    staggered(chunk(x, row) for x in range(sx) for row in range(first, last, 2))


def table_of(sy, refs):
    one, two, codes, one_h, two_h, codes_h = refs

    def table(x, row):
        if 0 <= row < sy:
            return one, two, codes, x * sy + row
        return one_h, two_h, codes_h, x * 4 + (row + 2 if row < 0 else row - sy + 2)

    return table


def apply_kernel(sx, sy, step, *refs):
    if step == 1:
        field, low, high_ = refs[:3]
        refs = refs[3:]

        def inner(x, row, group):
            return column(sx, sy, field, low, high_, x, row, group)

    else:
        previous = refs[0]
        refs = refs[1:]
        depth = 4 - step
        height = sy + 2 * depth

        def inner(x, row, group):
            return previous[pl.ds((x * height + row + depth) * ROWS + group, 8), :]

    from_low, from_high = refs[:2]
    table = table_of(sy, refs[2:8])
    leave_rows, middle_t_wide, enter_t_wide = refs[8:11]
    refs = refs[11:]
    before = 4 - step

    def get(x, row, group):
        if x < 0:
            return from_low[row + before]
        if x >= sx:
            return from_high[row + before]
        return inner(x, row, group)

    after = 3 - step
    height_out = sy + 2 * after
    if step < 3:
        image, to_low, to_high = refs

        def put(x, row, value):
            image[pl.ds((x * height_out + row + after) * ROWS, ROWS), :] = value
            if x == 0:
                to_low[row + after] = value[0:8]
            if x == sx - 1:
                to_high[row + after] = value[8:16]

        apply_rows(sx, -after, sy + after, get, table, leave_rows, middle_t_wide, enter_t_wide, put)
        return

    field, image_one, out = refs
    totals = [jnp.zeros((8, 128), F32) for _ in range(10)]

    def put(x, row, value):
        for group in (0, 8, 16):
            parts = (
                field[pl.ds((x * sy + row) * ROWS + group, 8), :],
                image_one[pl.ds((x * (sy + 4) + row + 2) * ROWS + group, 8), :],
                inner(x, row, group),
                value[group : group + 8],
            )
            at = 0
            for i in range(4):
                for j in range(i, 4):
                    totals[at] = totals[at] + parts[i] * parts[j]
                    at += 1

    apply_rows(sx, 0, sy, get, table, leave_rows, middle_t_wide, enter_t_wide, put)
    sums = jnp.concatenate(
        [jnp.sum(total, axis=0, keepdims=True) for total in totals] + [jnp.zeros((6, 128), F32)], axis=0
    )
    sums = jnp.broadcast_to(jnp.sum(sums, axis=1, keepdims=True), (16, 128))
    place = lax.broadcasted_iota(jnp.int32, (16, 128), 0) == lax.broadcasted_iota(jnp.int32, (16, 128), 1)
    line = jnp.sum(jnp.where(place, sums, 0.0), axis=0, keepdims=True)
    for i in range(out.shape[0]):
        out[i] = line


def least_squares(hess, target):
    rows = [list(line) for line in hess]
    target = list(target)
    for col in range(ITERS):
        upper = rows[col][col]
        lower = rows[col + 1][col]
        radius = jnp.sqrt(upper * upper + lower * lower)
        cosine = upper / radius
        sine = lower / radius
        for other in range(col, ITERS):
            first_value = rows[col][other]
            second_value = rows[col + 1][other]
            rows[col][other] = cosine * first_value + sine * second_value
            rows[col + 1][other] = cosine * second_value - sine * first_value
        first_value = target[col]
        second_value = target[col + 1]
        target[col] = cosine * first_value + sine * second_value
        target[col + 1] = cosine * second_value - sine * first_value
    coeffs = [None] * ITERS
    for col in reversed(range(ITERS)):
        accum = target[col]
        for other in range(col + 1, ITERS):
            accum = accum - rows[col][other] * coeffs[other]
        coeffs[col] = accum / rows[col][col]
    return coeffs


def finish_kernel(sx, sy, parts, gradient, image_one, image_two, out):
    total = parts[0]
    for i in range(1, parts.shape[0]):
        total = total + parts[i]
    total = jnp.broadcast_to(total, (8, 128))
    lane = lax.broadcasted_iota(jnp.int32, (8, 128), 1)
    gram = [[None] * 4 for _ in range(4)]
    at = 0
    for i in range(4):
        for j in range(i, 4):
            one = jnp.sum(jnp.where(lane == at, total, 0.0), axis=1, keepdims=True)
            gram[i][j] = gram[j][i] = jnp.broadcast_to(one, (8, 128))
            at += 1
    size = [jnp.sqrt(gram[i][i]) for i in range(4)]
    inverse = [1.0 / value for value in size]
    cosines = [[gram[i][j] * inverse[i] * inverse[j] for j in range(4)] for i in range(4)]
    zero = jnp.zeros((8, 128), F32)
    one = zero + 1.0
    lower = [[zero] * 4 for _ in range(4)]
    for i in range(4):
        for j in range(i + 1):
            value = one if i == j else cosines[i][j]
            for k in range(j):
                value = value - lower[i][k] * lower[j][k]
            lower[i][j] = jnp.sqrt(jnp.maximum(value, FLOOR)) if i == j else value / lower[j][j]
    hess = [[zero] * ITERS for _ in range(ITERS + 1)]
    for j in range(ITERS):
        ratio = SHRINK * size[j + 1] * inverse[j]
        for i in range(j + 2):
            hess[i][j] = lower[j][i] - ratio * lower[j + 1][i]
    coeffs = least_squares(hess, [one, zero, zero, zero])
    scaled = [coeffs[j] * size[0] * inverse[j] for j in range(ITERS)]
    for x in range(sx):
        for row, k in enumerate(ORDER):
            second = image_one[pl.ds((x * (sy + 4) + 2) * ROWS + row, sy, stride=ROWS), :]
            third = image_two[pl.ds((x * (sy + 2) + 1) * ROWS + row, sy, stride=ROWS), :]
            out[k, x] = scaled[0] * gradient[k, x] + scaled[1] * second + scaled[2] * third


def exchange(axis, to_low, to_high):
    count = lax.axis_size(axis)
    forward = [(i, i + 1) for i in range(count - 1)]
    backward = [(i + 1, i) for i in range(count - 1)]
    return lax.ppermute(to_high, axis, forward), lax.ppermute(to_low, axis, backward)


def per_device(gradient, steady_state, enter_weight, middle_weight, leave_weight, links):
    sx, sy, sz = gradient.shape[1:]
    own = sx * sy

    def bind(kernel, *static):
        def bound(*refs):
            kernel(*static, *refs)

        bound.__name__ = kernel.__name__
        return bound

    flat = (own * ROWS, sz)
    message = (sx * 5 * ROWS, sz)
    field, state, to_low, to_high = call(
        bind(prepare_kernel, sx, sy),
        [(flat, F32), (flat, F32), (message, F32), (message, F32)],
        gradient, steady_state, links,
    )
    low, high_ = exchange("gy", to_low, to_high)
    enter_rows, leave_rows, middle_wide, middle_t_wide, enter_t_wide = call(
        weights_kernel,
        [((HID, HID), BF16), ((HID, HID), BF16), ((2 * HID, 2 * HID), BF16), ((2 * HID, 2 * HID), BF16), ((64, 2 * HID), BF16)],
        enter_weight.T, middle_weight, leave_weight,
    )

    def tables(count):
        return [((count, HID, sz), F32), ((count, HID, sz), F32), ((count, ROWS, sz), F32)]

    own_table = call(bind(own_slopes_kernel, own), tables(own), state, enter_rows, middle_wide)
    to_low, to_high = call(
        bind(faces_kernel, sx, sy), [((sy + 6, 8, sz), F32)] * 2, field, low, high_, own_table[2]
    )
    from_low, from_high = exchange("gx", to_low, to_high)
    halo_table = call(
        bind(halo_slopes_kernel, sx), tables(sx * 4), low, high_, enter_rows, middle_wide
    )
    shared = (*own_table, *halo_table, leave_rows, middle_t_wide, enter_t_wide)

    def image_shapes(depth):
        height = sy + 2 * depth
        return [((sx * height * ROWS, sz), F32), ((height, 8, sz), F32), ((height, 8, sz), F32)]

    image_one, to_low, to_high = call(
        bind(apply_kernel, sx, sy, 1), image_shapes(2), field, low, high_, from_low, from_high, *shared
    )
    from_low, from_high = exchange("gx", to_low, to_high)
    image_two, to_low, to_high = call(
        bind(apply_kernel, sx, sy, 2), image_shapes(1), image_one, from_low, from_high, *shared
    )
    from_low, from_high = exchange("gx", to_low, to_high)
    count_y = lax.axis_size("gy")
    count_x = lax.axis_size("gx")

    def last_kernel(*refs):
        *refs, field, image_one, out = refs
        apply_kernel(sx, sy, 3, *refs, field, image_one, out)

    (line,) = call(
        last_kernel, [((count_y, 1, sz), F32)], image_two, from_low, from_high, *shared, field, image_one
    )
    line = jnp.sum(lax.all_to_all(line, "gy", 0, 0), axis=0, keepdims=True)
    parts = lax.all_to_all(jnp.broadcast_to(line, (count_x, 1, sz)), "gx", 0, 0)
    (adjoint,) = call(
        bind(finish_kernel, sx, sy), [(gradient.shape, F32)], parts, gradient, image_one, image_two
    )
    return adjoint


def solution(mesh):
    in_specs = (
        P(None, "gx", "gy", None),
        P(None, "gx", "gy", None),
        P(),
        P(),
        P(),
        P(None, "gx", "gy", None),
    )
    out_specs = P(None, "gx", "gy", None)
    return jax.shard_map(
        per_device, mesh=mesh, in_specs=in_specs, out_specs=out_specs, check_vma=False
    )
```

```python
import jax
import jax.numpy as jnp
from jax import lax
from jax.experimental import pallas as pl
from jax.experimental.pallas import tpu as pltpu
from jax.sharding import PartitionSpec as P

Q = 19
HID = 128
ITERS = 3
ROWS = 24
SHRINK = 16.0
FLOOR = 1e-10
VMEM_BYTES = 16 * 1024 * 1024
SPAN = 6
FACE = 5

ORDER = (0, 4, 6, 8, 10, 2, 12, 14, 1, 5, 7, 9, 11, 3, 13, 15, 16, 17, 18)

F32 = jnp.float32
BF16 = jnp.bfloat16
VM = pl.BlockSpec(memory_space=pltpu.VMEM)


def call(kernel, outs, *args):
    return pl.pallas_call(
        kernel,
        out_shape=[jax.ShapeDtypeStruct(shape, kind) for shape, kind in outs],
        in_specs=[VM] * len(args),
        out_specs=[VM] * len(outs),
        compiler_params=pltpu.CompilerParams(vmem_limit_bytes=VMEM_BYTES),
    )(*args)


def high(x):
    return x.astype(BF16).astype(F32)


def rows_dot(weights, x):
    top = high(x)
    stack = jnp.concatenate([top, top, x - top, jnp.zeros((8, x.shape[1]), F32)], axis=0)
    return jnp.dot(weights, stack.astype(BF16), preferred_element_type=F32)


def wide_dot(weights, x):
    top = x.astype(BF16)
    rest = (x - top.astype(F32)).astype(BF16)
    both = jnp.dot(weights, jnp.concatenate([top, rest], axis=0), preferred_element_type=F32)
    half = weights.shape[0] // 2
    return both[:half] + both[half:]


def together(chunks):
    chunks = list(chunks)
    for at in range(0, len(chunks), 4):
        running = chunks[at : at + 4]
        while running:
            running = [chunk for chunk in running if next(chunk, None)]


def weights_kernel(enter_t, middle, leave, enter_rows, leave_rows, middle_wide, middle_t_wide, enter_t_wide):
    def ordered(ref):
        rows = [ref[k : k + 1, :] for k in ORDER]
        return jnp.concatenate(rows + [jnp.zeros((ROWS - Q, HID), F32)], axis=0)

    def tall(rows):
        top = high(rows)
        stack = jnp.concatenate([top, rows - top, top, jnp.zeros((HID - 3 * ROWS, HID), F32)], axis=0)
        return stack.T.astype(BF16)

    def wide(mat):
        top = high(mat)
        rest = mat - top
        upper = jnp.concatenate([top, top], axis=1)
        lower = jnp.concatenate([rest, jnp.zeros_like(rest)], axis=1)
        return jnp.concatenate([upper, lower], axis=0).astype(BF16)

    enter = ordered(enter_t)
    enter_rows[...] = tall(enter)
    leave_rows[...] = tall(ordered(leave))
    middle_wide[...] = wide(middle[...])
    middle_t_wide[...] = wide(middle[...].T)
    scaled = enter * (1.0 / SHRINK)
    enter_t_wide[...] = wide(jnp.concatenate([scaled, jnp.zeros((8, HID), F32)], axis=0))


def prepare_kernel(sx, sy, *refs):
    sources, (field, state, to_low, to_high), (gradient, steady, links), sems = refs[:3], refs[3:7], refs[7:10], refs[10]
    copies = [
        pltpu.make_async_copy(source, target, sems.at[i])
        for i, (source, target) in enumerate(zip(sources, (gradient, steady, links)))
    ]
    for copy in copies:
        copy.start()
    blank = jnp.zeros((8, 128), F32)
    for x in range(sx):
        for y in range(sy):
            at = (x * sy + y) * ROWS + 16
            field[pl.ds(at, 8), :] = blank
            state[pl.ds(at, 8), :] = blank
    copies[0].wait()
    for x in range(sx):
        for row, k in enumerate(ORDER):
            field[pl.ds(x * sy * ROWS + row, sy, stride=ROWS), :] = gradient[k, x]
    copies[1].wait()
    copies[2].wait()
    for x in range(sx):
        for row, k in enumerate(ORDER):
            state[pl.ds(x * sy * ROWS + row, sy, stride=ROWS), :] = steady[k, x]
        for word in range(2):
            state[pl.ds(x * sy * ROWS + Q + word, sy, stride=ROWS), :] = links[word, x].astype(F32)
    at = 0
    for ref, depth in ((field, 3), (state, 2)):
        for x in range(sx):
            size = depth * ROWS
            to_low[pl.ds(at, size), :] = ref[pl.ds(x * sy * ROWS, size), :]
            to_high[pl.ds(at, size), :] = ref[pl.ds((x * sy + sy - depth) * ROWS, size), :]
            at += size


def sublane():
    return lax.broadcasted_iota(jnp.int32, (8, 128), 0)


def row_constants(values):
    row = sublane()
    out = jnp.zeros((8, 128), jnp.int32)
    for at, value in enumerate(values):
        out = jnp.where(row == at, value, out)
    return out


def codes_of(tail):
    word_0 = jnp.broadcast_to(tail[3:4, :].astype(jnp.int32), (8, 128))
    word_1 = jnp.broadcast_to(tail[4:5, :].astype(jnp.int32), (8, 128))
    solid = (word_1 & (1 << (18 - 10))) != 0
    codes = []
    for group in range(3):
        members = [ORDER[group * 8 + i] if group * 8 + i < Q else -1 for i in range(8)]
        second = row_constants([1 if k >= 10 else 0 for k in members])
        bit = row_constants([0 if k < 0 else 1 << (k % 10) for k in members])
        pad = row_constants([1 if k < 0 else 0 for k in members])
        word = jnp.where(second == 1, word_1, word_0)
        code = jnp.where((word & bit) != 0, 1.0, 0.0)
        codes.append(jnp.where(jnp.logical_or(solid, pad == 1), 2.0, code))
    return codes


def slopes_of(columns, enter_rows, middle_wide, slope_one, slope_two, codes):
    enter = enter_rows[:, 0:80]
    middle = middle_wide[...]

    def chunk(at):
        pair = [ref[pl.ds(offset, ROWS), :] for ref, offset in columns[at : at + 2]]
        hidden = jnp.tanh(rows_dot(enter, jnp.concatenate(pair, axis=1)))
        yield True
        one = 1.0 - hidden * hidden
        hidden = jnp.tanh(wide_dot(middle, hidden))
        yield True
        two = 1.0 - hidden * hidden
        for i in range(2):
            slope_one[at + i] = one[:, i * 128 : (i + 1) * 128]
            slope_two[at + i] = two[:, i * 128 : (i + 1) * 128]
            for group, code in enumerate(codes_of(pair[i][16:24, :])):
                codes[at + i, group * 8 : group * 8 + 8, :] = code

    together(chunk(at) for at in range(0, len(columns), 2))


def own_slopes_kernel(count, state, enter_rows, middle_wide, slope_one, slope_two, codes):
    columns = [(state, i * ROWS) for i in range(count)]
    slopes_of(columns, enter_rows, middle_wide, slope_one, slope_two, codes)


def halo_slopes_kernel(sx, low, high_, enter_rows, middle_wide, slope_one, slope_two, codes):
    columns = []
    for x in range(sx):
        for ref in (low, high_):
            for row in range(2):
                columns.append((ref, (sx * 3 + x * 2 + row) * ROWS))
    slopes_of(columns, enter_rows, middle_wide, slope_one, slope_two, codes)


def face_shape(height, sz):
    return (-(-(height * FACE + 8 - FACE) // 8) * 8, sz)


def face(out, at, rows):
    out[pl.ds(at * FACE, FACE), :] = rows[0:FACE]


def face_tail(height, *outs):
    for out in outs:
        used = height * FACE
        out[pl.ds(used, out.shape[0] - used), :] = jnp.zeros((out.shape[0] - used, out.shape[1]), F32)


def faces_kernel(sx, sy, field, low, high_, _, to_low, to_high):
    face_tail(sy + 6, to_low, to_high)
    for row in range(-3, sy + 3):
        for x, group, out in ((0, 0, to_low), (sx - 1, 8, to_high)):
            face(out, row + 3, column(sx, sy, field, low, high_, x, row, group))


def column(sx, sy, field, low, high_, x, row, group):
    if row < 0:
        return low[pl.ds((x * 3 + row + 3) * ROWS + group, 8), :]
    if row >= sy:
        return high_[pl.ds((x * 3 + row - sy) * ROWS + group, 8), :]
    return field[pl.ds((x * sy + row) * ROWS + group, 8), :]


def pull_column(get, code, x, row):
    at = sublane()
    straight = jnp.logical_or(at == 0, jnp.logical_or(at == 3, at == 4))
    first = jnp.logical_or(at == 3, at == 6)
    second = jnp.logical_or(at == 4, at == 7)
    own = [get(x, row, group) for group in (0, 8, 16)]
    out = []
    for group, step in ((0, 1), (8, -1)):
        value = jnp.where(straight, get(x + step, row, group), get(x, row + step, group))
        value = jnp.where(at == 1, get(x + step, row + step, group), value)
        value = jnp.where(at == 2, get(x + step, row - step, group), value)
        up = pltpu.roll(value, 127, 1)
        down = pltpu.roll(value, 1, 1)
        if step < 0:
            up, down = down, up
        out.append(jnp.where(first, up, jnp.where(second, down, value)))
    up = pltpu.roll(own[2], 127, 1)
    down = pltpu.roll(own[2], 1, 1)
    out.append(jnp.where(at == 0, up, jnp.where(at == 1, down, own[2])))
    swapped = jnp.where(at == 0, pltpu.roll(own[2], 7, 0), jnp.where(at == 1, pltpu.roll(own[2], 1, 0), own[2]))
    result = []
    for pulled, back, flag in zip(out, (own[1], own[0], swapped), (code(0), code(8), code(16))):
        result.append(jnp.where(flag == 0.0, pulled, jnp.where(flag == 1.0, back, 0.0)))
    return jnp.concatenate(result, axis=0)


def apply_rows(sx, first, last, get, table, leave_rows, middle_t_wide, enter_t_wide, put):
    leave = leave_rows[:, 0:80]
    middle = middle_t_wide[...]
    enter = enter_t_wide[...]

    def chunk(x, row):
        entries = [table(x, r) for r in range(row, min(row + SPAN, last))]
        reads = [
            pull_column(get, lambda g, codes=codes, at=at: codes[at, g : g + 8, :], x, row + i)
            for i, (_, _, codes, at) in enumerate(entries)
        ]
        read = jnp.concatenate(reads, axis=1)
        yield True
        carried = rows_dot(leave, read) * jnp.concatenate([two[at] for _, two, _, at in entries], axis=1)
        yield True
        carried = wide_dot(middle, carried) * jnp.concatenate([one[at] for one, _, _, at in entries], axis=1)
        yield True
        image = (0.5 / SHRINK) * read + wide_dot(enter, carried)[:ROWS]
        for i in range(len(entries)):
            put(x, row + i, image[:, i * 128 : (i + 1) * 128])

    together(chunk(x, row) for x in range(sx) for row in range(first, last, SPAN))


def table_of(sy, refs):
    one, two, codes, one_h, two_h, codes_h = refs

    def table(x, row):
        if 0 <= row < sy:
            return one, two, codes, x * sy + row
        return one_h, two_h, codes_h, x * 4 + (row + 2 if row < 0 else row - sy + 2)

    return table


def apply_kernel(sx, sy, step, *refs):
    if step == 1:
        field, low, high_ = refs[:3]
        refs = refs[3:]

        def inner(x, row, group):
            return column(sx, sy, field, low, high_, x, row, group)

    else:
        previous = refs[0]
        refs = refs[1:]
        depth = 4 - step
        height = sy + 2 * depth

        def inner(x, row, group):
            return previous[pl.ds((x * height + row + depth) * ROWS + group, 8), :]

    from_low, from_high = refs[:2]
    table = table_of(sy, refs[2:8])
    leave_rows, middle_t_wide, enter_t_wide = refs[8:11]
    refs = refs[11:]
    before = 4 - step

    def get(x, row, group):
        if x < 0:
            return from_low[pl.ds((row + before) * FACE, 8), :]
        if x >= sx:
            return from_high[pl.ds((row + before) * FACE, 8), :]
        return inner(x, row, group)

    after = 3 - step
    height_out = sy + 2 * after
    if step < 3:
        image, to_low, to_high = refs
        face_tail(height_out, to_low, to_high)

        def put(x, row, value):
            image[pl.ds((x * height_out + row + after) * ROWS, ROWS), :] = value
            if x == 0:
                face(to_low, row + after, value[0:8])
            if x == sx - 1:
                face(to_high, row + after, value[8:16])

        apply_rows(sx, -after, sy + after, get, table, leave_rows, middle_t_wide, enter_t_wide, put)
        return

    field, image_one, out = refs
    totals = [jnp.zeros((8, 128), F32) for _ in range(10)]

    def put(x, row, value):
        for group in (0, 8, 16):
            parts = (
                field[pl.ds((x * sy + row) * ROWS + group, 8), :],
                image_one[pl.ds((x * (sy + 4) + row + 2) * ROWS + group, 8), :],
                inner(x, row, group),
                value[group : group + 8],
            )
            at = 0
            for i in range(4):
                for j in range(i, 4):
                    totals[at] = totals[at] + parts[i] * parts[j]
                    at += 1

    apply_rows(sx, 0, sy, get, table, leave_rows, middle_t_wide, enter_t_wide, put)
    sums = jnp.concatenate(
        [jnp.sum(total, axis=0, keepdims=True) for total in totals] + [jnp.zeros((6, 128), F32)], axis=0
    )
    sums = jnp.broadcast_to(jnp.sum(sums, axis=1, keepdims=True), (16, 128))
    place = lax.broadcasted_iota(jnp.int32, (16, 128), 0) == lax.broadcasted_iota(jnp.int32, (16, 128), 1)
    line = jnp.sum(jnp.where(place, sums, 0.0), axis=0, keepdims=True)
    for i in range(out.shape[0]):
        out[i] = line


def least_squares(hess, target):
    rows = [list(line) for line in hess]
    target = list(target)
    for col in range(ITERS):
        upper = rows[col][col]
        lower = rows[col + 1][col]
        radius = jnp.sqrt(upper * upper + lower * lower)
        cosine = upper / radius
        sine = lower / radius
        for other in range(col, ITERS):
            first_value = rows[col][other]
            second_value = rows[col + 1][other]
            rows[col][other] = cosine * first_value + sine * second_value
            rows[col + 1][other] = cosine * second_value - sine * first_value
        first_value = target[col]
        second_value = target[col + 1]
        target[col] = cosine * first_value + sine * second_value
        target[col + 1] = cosine * second_value - sine * first_value
    coeffs = [None] * ITERS
    for col in reversed(range(ITERS)):
        accum = target[col]
        for other in range(col + 1, ITERS):
            accum = accum - rows[col][other] * coeffs[other]
        coeffs[col] = accum / rows[col][col]
    return coeffs


def finish_kernel(sx, sy, parts, gradient, image_one, image_two, out):
    total = parts[0]
    for i in range(1, parts.shape[0]):
        total = total + parts[i]
    total = jnp.broadcast_to(total, (8, 128))
    lane = lax.broadcasted_iota(jnp.int32, (8, 128), 1)
    gram = [[None] * 4 for _ in range(4)]
    at = 0
    for i in range(4):
        for j in range(i, 4):
            one = jnp.sum(jnp.where(lane == at, total, 0.0), axis=1, keepdims=True)
            gram[i][j] = gram[j][i] = jnp.broadcast_to(one, (8, 128))
            at += 1
    size = [jnp.sqrt(gram[i][i]) for i in range(4)]
    inverse = [1.0 / value for value in size]
    cosines = [[gram[i][j] * inverse[i] * inverse[j] for j in range(4)] for i in range(4)]
    zero = jnp.zeros((8, 128), F32)
    one = zero + 1.0
    lower = [[zero] * 4 for _ in range(4)]
    for i in range(4):
        for j in range(i + 1):
            value = one if i == j else cosines[i][j]
            for k in range(j):
                value = value - lower[i][k] * lower[j][k]
            lower[i][j] = jnp.sqrt(jnp.maximum(value, FLOOR)) if i == j else value / lower[j][j]
    hess = [[zero] * ITERS for _ in range(ITERS + 1)]
    for j in range(ITERS):
        ratio = SHRINK * size[j + 1] * inverse[j]
        for i in range(j + 2):
            hess[i][j] = lower[j][i] - ratio * lower[j + 1][i]
    coeffs = least_squares(hess, [one, zero, zero, zero])
    scaled = [coeffs[j] * size[0] * inverse[j] for j in range(ITERS)]
    for x in range(sx):
        for row, k in enumerate(ORDER):
            second = image_one[pl.ds((x * (sy + 4) + 2) * ROWS + row, sy, stride=ROWS), :]
            third = image_two[pl.ds((x * (sy + 2) + 1) * ROWS + row, sy, stride=ROWS), :]
            out[k, x] = scaled[0] * gradient[k, x] + scaled[1] * second + scaled[2] * third


def exchange(axis, to_low, to_high):
    count = lax.axis_size(axis)
    forward = [(i, i + 1) for i in range(count - 1)]
    backward = [(i + 1, i) for i in range(count - 1)]
    return lax.ppermute(to_high, axis, forward), lax.ppermute(to_low, axis, backward)


def per_device(gradient, steady_state, enter_weight, middle_weight, leave_weight, links):
    sx, sy, sz = gradient.shape[1:]
    own = sx * sy

    def bind(kernel, *static):
        def bound(*refs):
            kernel(*static, *refs)

        bound.__name__ = kernel.__name__
        return bound

    flat = (own * ROWS, sz)
    message = (sx * 5 * ROWS, sz)
    field, state, to_low, to_high = pl.pallas_call(
        bind(prepare_kernel, sx, sy),
        out_shape=[jax.ShapeDtypeStruct(shape, F32) for shape in (flat, flat, message, message)],
        in_specs=[pl.BlockSpec(memory_space=pltpu.HBM)] * 3,
        out_specs=[VM] * 4,
        scratch_shapes=[pltpu.VMEM(x.shape, x.dtype) for x in (gradient, steady_state, links)]
        + [pltpu.SemaphoreType.DMA((3,))],
        compiler_params=pltpu.CompilerParams(vmem_limit_bytes=VMEM_BYTES),
    )(gradient, steady_state, links)
    low, high_ = exchange("gy", to_low, to_high)
    enter_rows, leave_rows, middle_wide, middle_t_wide, enter_t_wide = call(
        weights_kernel,
        [((HID, HID), BF16), ((HID, HID), BF16), ((2 * HID, 2 * HID), BF16), ((2 * HID, 2 * HID), BF16), ((64, 2 * HID), BF16)],
        enter_weight.T, middle_weight, leave_weight,
    )

    def tables(count):
        return [((count, HID, sz), F32), ((count, HID, sz), F32), ((count, ROWS, sz), F32)]

    own_table = call(bind(own_slopes_kernel, own), tables(own), state, enter_rows, middle_wide)
    to_low, to_high = call(
        bind(faces_kernel, sx, sy), [(face_shape(sy + 6, sz), F32)] * 2, field, low, high_, own_table[2]
    )
    from_low, from_high = exchange("gx", to_low, to_high)
    halo_table = call(
        bind(halo_slopes_kernel, sx), tables(sx * 4), low, high_, enter_rows, middle_wide
    )
    shared = (*own_table, *halo_table, leave_rows, middle_t_wide, enter_t_wide)

    def image_shapes(depth):
        height = sy + 2 * depth
        return [((sx * height * ROWS, sz), F32), (face_shape(height, sz), F32), (face_shape(height, sz), F32)]

    image_one, to_low, to_high = call(
        bind(apply_kernel, sx, sy, 1), image_shapes(2), field, low, high_, from_low, from_high, *shared
    )
    from_low, from_high = exchange("gx", to_low, to_high)
    image_two, to_low, to_high = call(
        bind(apply_kernel, sx, sy, 2), image_shapes(1), image_one, from_low, from_high, *shared
    )
    from_low, from_high = exchange("gx", to_low, to_high)
    count_y = lax.axis_size("gy")
    count_x = lax.axis_size("gx")

    def last_kernel(*refs):
        *refs, field, image_one, out = refs
        apply_kernel(sx, sy, 3, *refs, field, image_one, out)

    (line,) = call(
        last_kernel, [((count_y, 1, sz), F32)], image_two, from_low, from_high, *shared, field, image_one
    )
    line = jnp.sum(lax.all_to_all(line, "gy", 0, 0), axis=0, keepdims=True)
    parts = lax.all_to_all(jnp.broadcast_to(line, (count_x, 1, sz)), "gx", 0, 0)
    (adjoint,) = call(
        bind(finish_kernel, sx, sy), [(gradient.shape, F32)], parts, gradient, image_one, image_two
    )
    return adjoint


def solution(mesh):
    in_specs = (
        P(None, "gx", "gy", None),
        P(None, "gx", "gy", None),
        P(),
        P(),
        P(),
        P(None, "gx", "gy", None),
    )
    out_specs = P(None, "gx", "gy", None)
    return jax.shard_map(
        per_device, mesh=mesh, in_specs=in_specs, out_specs=out_specs, check_vma=False
    )
```

```python
import jax
import jax.numpy as jnp
from jax import lax
from jax.experimental import pallas as pl
from jax.experimental.pallas import tpu as pltpu
from jax.sharding import PartitionSpec as P

Q = 19
HID = 128
ITERS = 3
ROWS = 24
SHRINK = 16.0
FLOOR = 1e-10
VMEM_BYTES = 16 * 1024 * 1024
SPAN = 6
FACE = 5

ORDER = (0, 4, 6, 8, 10, 2, 12, 14, 1, 5, 7, 9, 11, 3, 13, 15, 16, 17, 18)

F32 = jnp.float32
BF16 = jnp.bfloat16
VM = pl.BlockSpec(memory_space=pltpu.VMEM)
SM = pl.BlockSpec(memory_space=pltpu.SMEM)


def call(kernel, outs, *args):
    return pl.pallas_call(
        kernel,
        out_shape=[jax.ShapeDtypeStruct(shape, kind) for shape, kind in outs],
        in_specs=[SM if x.shape == (1,) else VM for x in args],
        out_specs=[VM] * len(outs),
        compiler_params=pltpu.CompilerParams(vmem_limit_bytes=VMEM_BYTES),
    )(*args)


def high(x):
    return x.astype(BF16).astype(F32)


def rows_dot(weights, x):
    top = high(x)
    stack = jnp.concatenate([top, top, x - top, jnp.zeros((8, x.shape[1]), F32)], axis=0)
    return jnp.dot(weights, stack.astype(BF16), preferred_element_type=F32)


def wide_dot(weights, x):
    top = x.astype(BF16)
    rest = (x - top.astype(F32)).astype(BF16)
    both = jnp.dot(weights, jnp.concatenate([top, rest], axis=0), preferred_element_type=F32)
    half = weights.shape[0] // 2
    return both[:half] + both[half:]


def together(chunks):
    chunks = list(chunks)
    for at in range(0, len(chunks), 4):
        running = chunks[at : at + 4]
        while running:
            running = [chunk for chunk in running if next(chunk, None)]


def weights_kernel(enter_t, middle, leave, enter_rows, leave_rows, middle_wide, middle_t_wide, enter_t_wide):
    def ordered(ref):
        rows = [ref[k : k + 1, :] for k in ORDER]
        return jnp.concatenate(rows + [jnp.zeros((ROWS - Q, HID), F32)], axis=0)

    def tall(rows):
        top = high(rows)
        stack = jnp.concatenate([top, rows - top, top, jnp.zeros((HID - 3 * ROWS, HID), F32)], axis=0)
        return stack.T.astype(BF16)

    def wide(mat):
        top = high(mat)
        rest = mat - top
        upper = jnp.concatenate([top, top], axis=1)
        lower = jnp.concatenate([rest, jnp.zeros_like(rest)], axis=1)
        return jnp.concatenate([upper, lower], axis=0).astype(BF16)

    enter = ordered(enter_t)
    enter_rows[...] = tall(enter)
    leave_rows[...] = tall(ordered(leave))
    middle_wide[...] = wide(middle[...])
    middle_t_wide[...] = wide(middle[...].T)
    scaled = enter * (1.0 / SHRINK)
    enter_t_wide[...] = wide(jnp.concatenate([scaled, jnp.zeros((8, HID), F32)], axis=0))


def offset_by(odd, low, high_):
    first = pl.multiple_of(jnp.where(odd, low, high_), 8)
    second = pl.multiple_of(jnp.where(odd, high_, low), 8)
    return first, second


def prepare_kernel(sx, sy, *refs):
    sources, (field, state, to_first, to_second), refs = refs[:3], refs[4:8], (refs[3], *refs[8:])
    odd, gradient, steady, links, sems = refs
    odd = odd[0] == 1
    copies = [
        pltpu.make_async_copy(source, target, sems.at[i])
        for i, (source, target) in enumerate(zip(sources, (gradient, steady, links)))
    ]
    for copy in copies:
        copy.start()
    blank = jnp.zeros((8, 128), F32)
    for x in range(sx):
        for y in range(sy):
            at = (x * sy + y) * ROWS + 16
            field[pl.ds(at, 8), :] = blank
            state[pl.ds(at, 8), :] = blank
    copies[0].wait()
    for x in range(sx):
        for row, k in enumerate(ORDER):
            field[pl.ds(x * sy * ROWS + row, sy, stride=ROWS), :] = gradient[k, x]
    copies[1].wait()
    copies[2].wait()
    for x in range(sx):
        for row, k in enumerate(ORDER):
            state[pl.ds(x * sy * ROWS + row, sy, stride=ROWS), :] = steady[k, x]
        for word in range(2):
            state[pl.ds(x * sy * ROWS + Q + word, sy, stride=ROWS), :] = links[word, x].astype(F32)
    at = 0
    for ref, depth in ((field, 3), (state, 2)):
        for x in range(sx):
            size = depth * ROWS
            first, second = offset_by(odd, x * sy * ROWS, (x * sy + sy - depth) * ROWS)
            to_first[pl.ds(at, size), :] = ref[pl.ds(first, size), :]
            to_second[pl.ds(at, size), :] = ref[pl.ds(second, size), :]
            at += size


def sublane():
    return lax.broadcasted_iota(jnp.int32, (8, 128), 0)


def row_constants(values):
    row = sublane()
    out = jnp.zeros((8, 128), jnp.int32)
    for at, value in enumerate(values):
        out = jnp.where(row == at, value, out)
    return out


def codes_of(tail):
    word_0 = jnp.broadcast_to(tail[3:4, :].astype(jnp.int32), (8, 128))
    word_1 = jnp.broadcast_to(tail[4:5, :].astype(jnp.int32), (8, 128))
    solid = (word_1 & (1 << (18 - 10))) != 0
    codes = []
    for group in range(3):
        members = [ORDER[group * 8 + i] if group * 8 + i < Q else -1 for i in range(8)]
        second = row_constants([1 if k >= 10 else 0 for k in members])
        bit = row_constants([0 if k < 0 else 1 << (k % 10) for k in members])
        pad = row_constants([1 if k < 0 else 0 for k in members])
        word = jnp.where(second == 1, word_1, word_0)
        code = jnp.where((word & bit) != 0, 1.0, 0.0)
        codes.append(jnp.where(jnp.logical_or(solid, pad == 1), 2.0, code))
    return codes


def slopes_of(columns, enter_rows, middle_wide, slope_one, slope_two, codes):
    enter = enter_rows[:, 0:80]
    middle = middle_wide[...]

    def chunk(at):
        pair = [ref[pl.ds(offset, ROWS), :] for ref, offset in columns[at : at + 2]]
        hidden = jnp.tanh(rows_dot(enter, jnp.concatenate(pair, axis=1)))
        yield True
        one = 1.0 - hidden * hidden
        hidden = jnp.tanh(wide_dot(middle, hidden))
        yield True
        two = 1.0 - hidden * hidden
        for i in range(2):
            slope_one[at + i] = one[:, i * 128 : (i + 1) * 128]
            slope_two[at + i] = two[:, i * 128 : (i + 1) * 128]
            for group, code in enumerate(codes_of(pair[i][16:24, :])):
                codes[at + i, group * 8 : group * 8 + 8, :] = code

    together(chunk(at) for at in range(0, len(columns), 2))


def own_slopes_kernel(count, state, enter_rows, middle_wide, slope_one, slope_two, codes):
    columns = [(state, i * ROWS) for i in range(count)]
    slopes_of(columns, enter_rows, middle_wide, slope_one, slope_two, codes)


def halo_slopes_kernel(sx, low, high_, enter_rows, middle_wide, slope_one, slope_two, codes):
    columns = []
    for x in range(sx):
        for ref in (low, high_):
            for row in range(2):
                columns.append((ref, (sx * 3 + x * 2 + row) * ROWS))
    slopes_of(columns, enter_rows, middle_wide, slope_one, slope_two, codes)


def face_shape(height, sz):
    return (-(-(height * FACE + 8 - FACE) // 8) * 8, sz)


def face(out, at, rows):
    out[pl.ds(at * FACE, FACE), :] = rows[0:FACE]


def face_tail(height, *outs):
    for out in outs:
        used = height * FACE
        out[pl.ds(used, out.shape[0] - used), :] = jnp.zeros((out.shape[0] - used, out.shape[1]), F32)


def faces_kernel(sx, sy, odd_x, odd_y, field, first, second, _, low, high_, to_first, to_second):
    odd = jnp.full((8, 128), odd_y[0]) == 1
    for at in range(0, first.shape[0], 8):
        one, two = first[pl.ds(at, 8), :], second[pl.ds(at, 8), :]
        low[pl.ds(at, 8), :] = jnp.where(odd, one, two)
        high_[pl.ds(at, 8), :] = jnp.where(odd, two, one)
    face_tail(sy + 6, to_first, to_second)
    odd = jnp.full((8, 128), odd_x[0]) == 1
    for row in range(-3, sy + 3):
        down = column(sx, sy, field, low, high_, 0, row, 0)
        up = column(sx, sy, field, low, high_, sx - 1, row, 8)
        face(to_first, row + 3, jnp.where(odd, down, up))
        face(to_second, row + 3, jnp.where(odd, up, down))


def column(sx, sy, field, low, high_, x, row, group):
    if row < 0:
        return low[pl.ds((x * 3 + row + 3) * ROWS + group, 8), :]
    if row >= sy:
        return high_[pl.ds((x * 3 + row - sy) * ROWS + group, 8), :]
    return field[pl.ds((x * sy + row) * ROWS + group, 8), :]


def pull_column(get, code, x, row):
    at = sublane()
    straight = jnp.logical_or(at == 0, jnp.logical_or(at == 3, at == 4))
    first = jnp.logical_or(at == 3, at == 6)
    second = jnp.logical_or(at == 4, at == 7)
    own = [get(x, row, group) for group in (0, 8, 16)]
    out = []
    for group, step in ((0, 1), (8, -1)):
        value = jnp.where(straight, get(x + step, row, group), get(x, row + step, group))
        value = jnp.where(at == 1, get(x + step, row + step, group), value)
        value = jnp.where(at == 2, get(x + step, row - step, group), value)
        up = pltpu.roll(value, 127, 1)
        down = pltpu.roll(value, 1, 1)
        if step < 0:
            up, down = down, up
        out.append(jnp.where(first, up, jnp.where(second, down, value)))
    up = pltpu.roll(own[2], 127, 1)
    down = pltpu.roll(own[2], 1, 1)
    out.append(jnp.where(at == 0, up, jnp.where(at == 1, down, own[2])))
    swapped = jnp.where(at == 0, pltpu.roll(own[2], 7, 0), jnp.where(at == 1, pltpu.roll(own[2], 1, 0), own[2]))
    result = []
    for pulled, back, flag in zip(out, (own[1], own[0], swapped), (code(0), code(8), code(16))):
        result.append(jnp.where(flag == 0.0, pulled, jnp.where(flag == 1.0, back, 0.0)))
    return jnp.concatenate(result, axis=0)


def apply_rows(sx, first, last, get, table, leave_rows, middle_t_wide, enter_t_wide, put):
    leave = leave_rows[:, 0:80]
    middle = middle_t_wide[...]
    enter = enter_t_wide[...]

    def chunk(x, row):
        entries = [table(x, r) for r in range(row, min(row + SPAN, last))]
        reads = [
            pull_column(get, lambda g, codes=codes, at=at: codes[at, g : g + 8, :], x, row + i)
            for i, (_, _, codes, at) in enumerate(entries)
        ]
        read = jnp.concatenate(reads, axis=1)
        yield True
        carried = rows_dot(leave, read) * jnp.concatenate([two[at] for _, two, _, at in entries], axis=1)
        yield True
        carried = wide_dot(middle, carried) * jnp.concatenate([one[at] for one, _, _, at in entries], axis=1)
        yield True
        image = (0.5 / SHRINK) * read + wide_dot(enter, carried)[:ROWS]
        for i in range(len(entries)):
            put(x, row + i, image[:, i * 128 : (i + 1) * 128])

    together(chunk(x, row) for x in range(sx) for row in range(first, last, SPAN))


def table_of(sy, refs):
    one, two, codes, one_h, two_h, codes_h = refs

    def table(x, row):
        if 0 <= row < sy:
            return one, two, codes, x * sy + row
        return one_h, two_h, codes_h, x * 4 + (row + 2 if row < 0 else row - sy + 2)

    return table


def apply_kernel(sx, sy, step, *refs):
    odd_x, *refs = refs
    odd = jnp.full((8, 128), odd_x[0]) == 1
    if step == 1:
        field, low, high_ = refs[:3]
        refs = refs[3:]

        def inner(x, row, group):
            return column(sx, sy, field, low, high_, x, row, group)

    else:
        previous = refs[0]
        refs = refs[1:]
        depth = 4 - step
        height = sy + 2 * depth

        def inner(x, row, group):
            return previous[pl.ds((x * height + row + depth) * ROWS + group, 8), :]

    first, second = refs[:2]
    table = table_of(sy, refs[2:8])
    leave_rows, middle_t_wide, enter_t_wide = refs[8:11]
    refs = refs[11:]
    before = 4 - step
    seen = {}

    def beside(row):
        if row not in seen:
            one = first[pl.ds((row + before) * FACE, 8), :]
            two = second[pl.ds((row + before) * FACE, 8), :]
            seen[row] = jnp.where(odd, one, two), jnp.where(odd, two, one)
        return seen[row]

    def get(x, row, group):
        if x < 0:
            return beside(row)[0]
        if x >= sx:
            return beside(row)[1]
        return inner(x, row, group)

    after = 3 - step
    height_out = sy + 2 * after
    if step < 3:
        image, to_first, to_second = refs
        face_tail(height_out, to_first, to_second)

        def put(x, row, value):
            image[pl.ds((x * height_out + row + after) * ROWS, ROWS), :] = value

        apply_rows(sx, -after, sy + after, get, table, leave_rows, middle_t_wide, enter_t_wide, put)
        one, two = offset_by(odd_x[0] == 1, 0, (sx - 1) * height_out * ROWS + 8)
        for row in range(height_out):
            face(to_first, row, image[pl.ds(one + row * ROWS, 8), :])
            face(to_second, row, image[pl.ds(two + row * ROWS, 8), :])
        return

    field, image_one, out = refs
    totals = [jnp.zeros((8, 128), F32) for _ in range(10)]

    def put(x, row, value):
        for group in (0, 8, 16):
            parts = (
                field[pl.ds((x * sy + row) * ROWS + group, 8), :],
                image_one[pl.ds((x * (sy + 4) + row + 2) * ROWS + group, 8), :],
                inner(x, row, group),
                value[group : group + 8],
            )
            at = 0
            for i in range(4):
                for j in range(i, 4):
                    totals[at] = totals[at] + parts[i] * parts[j]
                    at += 1

    apply_rows(sx, 0, sy, get, table, leave_rows, middle_t_wide, enter_t_wide, put)
    sums = jnp.concatenate(
        [jnp.sum(total, axis=0, keepdims=True) for total in totals] + [jnp.zeros((6, 128), F32)], axis=0
    )
    sums = jnp.broadcast_to(jnp.sum(sums, axis=1, keepdims=True), (16, 128))
    place = lax.broadcasted_iota(jnp.int32, (16, 128), 0) == lax.broadcasted_iota(jnp.int32, (16, 128), 1)
    line = jnp.sum(jnp.where(place, sums, 0.0), axis=0, keepdims=True)
    for i in range(out.shape[0]):
        out[i] = line


def least_squares(hess, target):
    rows = [list(line) for line in hess]
    target = list(target)
    for col in range(ITERS):
        upper = rows[col][col]
        lower = rows[col + 1][col]
        radius = jnp.sqrt(upper * upper + lower * lower)
        cosine = upper / radius
        sine = lower / radius
        for other in range(col, ITERS):
            first_value = rows[col][other]
            second_value = rows[col + 1][other]
            rows[col][other] = cosine * first_value + sine * second_value
            rows[col + 1][other] = cosine * second_value - sine * first_value
        first_value = target[col]
        second_value = target[col + 1]
        target[col] = cosine * first_value + sine * second_value
        target[col + 1] = cosine * second_value - sine * first_value
    coeffs = [None] * ITERS
    for col in reversed(range(ITERS)):
        accum = target[col]
        for other in range(col + 1, ITERS):
            accum = accum - rows[col][other] * coeffs[other]
        coeffs[col] = accum / rows[col][col]
    return coeffs


def finish_kernel(sx, sy, parts, gradient, image_one, image_two, out):
    total = parts[0]
    for i in range(1, parts.shape[0]):
        total = total + parts[i]
    total = jnp.broadcast_to(total, (8, 128))
    lane = lax.broadcasted_iota(jnp.int32, (8, 128), 1)
    gram = [[None] * 4 for _ in range(4)]
    at = 0
    for i in range(4):
        for j in range(i, 4):
            one = jnp.sum(jnp.where(lane == at, total, 0.0), axis=1, keepdims=True)
            gram[i][j] = gram[j][i] = jnp.broadcast_to(one, (8, 128))
            at += 1
    size = [jnp.sqrt(gram[i][i]) for i in range(4)]
    inverse = [1.0 / value for value in size]
    cosines = [[gram[i][j] * inverse[i] * inverse[j] for j in range(4)] for i in range(4)]
    zero = jnp.zeros((8, 128), F32)
    one = zero + 1.0
    lower = [[zero] * 4 for _ in range(4)]
    for i in range(4):
        for j in range(i + 1):
            value = one if i == j else cosines[i][j]
            for k in range(j):
                value = value - lower[i][k] * lower[j][k]
            lower[i][j] = jnp.sqrt(jnp.maximum(value, FLOOR)) if i == j else value / lower[j][j]
    hess = [[zero] * ITERS for _ in range(ITERS + 1)]
    for j in range(ITERS):
        ratio = SHRINK * size[j + 1] * inverse[j]
        for i in range(j + 2):
            hess[i][j] = lower[j][i] - ratio * lower[j + 1][i]
    coeffs = least_squares(hess, [one, zero, zero, zero])
    scaled = [coeffs[j] * size[0] * inverse[j] for j in range(ITERS)]
    for x in range(sx):
        for row, k in enumerate(ORDER):
            second = image_one[pl.ds((x * (sy + 4) + 2) * ROWS + row, sy, stride=ROWS), :]
            third = image_two[pl.ds((x * (sy + 2) + 1) * ROWS + row, sy, stride=ROWS), :]
            out[k, x] = scaled[0] * gradient[k, x] + scaled[1] * second + scaled[2] * third


def exchange(axis, to_first, to_second):
    count = lax.axis_size(axis)
    near = [(i, i ^ 1) for i in range(count)]
    far = [(i, ((i + 1) ^ 1) - 1) for i in range(1, count - 1)]
    first = lax.ppermute(to_first, axis, near)
    second = lax.ppermute(to_second, axis, far)
    return first, second


def per_device(gradient, steady_state, enter_weight, middle_weight, leave_weight, links):
    sx, sy, sz = gradient.shape[1:]
    own = sx * sy
    odd_x, odd_y = [(lax.axis_index(axis) % 2).reshape(1) for axis in ("gx", "gy")]

    def bind(kernel, *static):
        def bound(*refs):
            kernel(*static, *refs)

        bound.__name__ = kernel.__name__
        return bound

    flat = (own * ROWS, sz)
    message = (sx * 5 * ROWS, sz)
    field, state, to_first, to_second = pl.pallas_call(
        bind(prepare_kernel, sx, sy),
        out_shape=[jax.ShapeDtypeStruct(shape, F32) for shape in (flat, flat, message, message)],
        in_specs=[pl.BlockSpec(memory_space=pltpu.HBM)] * 3 + [SM],
        out_specs=[VM] * 4,
        scratch_shapes=[pltpu.VMEM(x.shape, x.dtype) for x in (gradient, steady_state, links)]
        + [pltpu.SemaphoreType.DMA((3,))],
        compiler_params=pltpu.CompilerParams(vmem_limit_bytes=VMEM_BYTES),
    )(gradient, steady_state, links, odd_y)
    first, second = exchange("gy", to_first, to_second)
    enter_rows, leave_rows, middle_wide, middle_t_wide, enter_t_wide = call(
        weights_kernel,
        [((HID, HID), BF16), ((HID, HID), BF16), ((2 * HID, 2 * HID), BF16), ((2 * HID, 2 * HID), BF16), ((64, 2 * HID), BF16)],
        enter_weight.T, middle_weight, leave_weight,
    )

    def tables(count):
        return [((count, HID, sz), F32), ((count, HID, sz), F32), ((count, ROWS, sz), F32)]

    own_table = call(bind(own_slopes_kernel, own), tables(own), state, enter_rows, middle_wide)
    low, high_, to_first, to_second = call(
        bind(faces_kernel, sx, sy),
        [(message, F32)] * 2 + [(face_shape(sy + 6, sz), F32)] * 2,
        odd_x, odd_y, field, first, second, own_table[2],
    )
    first, second = exchange("gx", to_first, to_second)
    halo_table = call(
        bind(halo_slopes_kernel, sx), tables(sx * 4), low, high_, enter_rows, middle_wide
    )
    shared = (*own_table, *halo_table, leave_rows, middle_t_wide, enter_t_wide)

    def image_shapes(depth):
        height = sy + 2 * depth
        return [((sx * height * ROWS, sz), F32), (face_shape(height, sz), F32), (face_shape(height, sz), F32)]

    image_one, to_first, to_second = call(
        bind(apply_kernel, sx, sy, 1), image_shapes(2), odd_x, field, low, high_, first, second, *shared
    )
    first, second = exchange("gx", to_first, to_second)
    image_two, to_first, to_second = call(
        bind(apply_kernel, sx, sy, 2), image_shapes(1), odd_x, image_one, first, second, *shared
    )
    first, second = exchange("gx", to_first, to_second)
    count_y = lax.axis_size("gy")
    count_x = lax.axis_size("gx")

    def last_kernel(*refs):
        *refs, field, image_one, out = refs
        apply_kernel(sx, sy, 3, *refs, field, image_one, out)

    (line,) = call(
        last_kernel, [((count_y, 1, sz), F32)], odd_x, image_two, first, second, *shared, field, image_one
    )
    line = jnp.sum(lax.all_to_all(line, "gy", 0, 0), axis=0, keepdims=True)
    parts = lax.all_to_all(jnp.broadcast_to(line, (count_x, 1, sz)), "gx", 0, 0)
    (adjoint,) = call(
        bind(finish_kernel, sx, sy), [(gradient.shape, F32)], parts, gradient, image_one, image_two
    )
    return adjoint


def solution(mesh):
    in_specs = (
        P(None, "gx", "gy", None),
        P(None, "gx", "gy", None),
        P(),
        P(),
        P(),
        P(None, "gx", "gy", None),
    )
    out_specs = P(None, "gx", "gy", None)
    return jax.shard_map(
        per_device, mesh=mesh, in_specs=in_specs, out_specs=out_specs, check_vma=False
    )
```

```python
import jax
import jax.numpy as jnp
from jax import lax
from jax.experimental import pallas as pl
from jax.experimental.pallas import tpu as pltpu
from jax.sharding import PartitionSpec as P


Q = 19
HID = 128
ITERS = 3
ROWS = 24
SHRINK = 16.0
FLOOR = 1e-10
VMEM_BYTES = 16 * 1024 * 1024
SPAN = 6
FACE = 5

ORDER = (0, 4, 6, 8, 10, 2, 12, 14, 1, 5, 7, 9, 11, 3, 13, 15, 16, 17, 18)

F32 = jnp.float32
BF16 = jnp.bfloat16
VM = pl.BlockSpec(memory_space=pltpu.VMEM)
SM = pl.BlockSpec(memory_space=pltpu.SMEM)


def call(kernel, outs, *args):
    return pl.pallas_call(
        kernel,
        out_shape=[jax.ShapeDtypeStruct(shape, kind) for shape, kind in outs],
        in_specs=[SM if x.shape == (1,) else VM for x in args],
        out_specs=[VM] * len(outs),
        compiler_params=pltpu.CompilerParams(vmem_limit_bytes=VMEM_BYTES),
    )(*args)


def high(x):
    return x.astype(BF16).astype(F32)


def rows_dot(weights, x):
    top = high(x)
    stack = jnp.concatenate([top, top, x - top, jnp.zeros((8, x.shape[1]), F32)], axis=0)
    return jnp.dot(weights, stack.astype(BF16), preferred_element_type=F32)


def wide_dot(weights, x):
    top = x.astype(BF16)
    rest = (x - top.astype(F32)).astype(BF16)
    both = jnp.dot(weights, jnp.concatenate([top, rest], axis=0), preferred_element_type=F32)
    half = weights.shape[0] // 2
    return both[:half] + both[half:]


def together(chunks):
    chunks = list(chunks)
    for at in range(0, len(chunks), 4):
        running = chunks[at : at + 4]
        while running:
            running = [chunk for chunk in running if next(chunk, None)]


def weights_kernel(enter_t, middle, leave, enter_rows, leave_rows, middle_wide, middle_t_wide, enter_t_wide):
    def ordered(ref):
        rows = [ref[k : k + 1, :] for k in ORDER]
        return jnp.concatenate(rows + [jnp.zeros((ROWS - Q, HID), F32)], axis=0)

    def tall(rows):
        top = high(rows)
        stack = jnp.concatenate([top, rows - top, top, jnp.zeros((HID - 3 * ROWS, HID), F32)], axis=0)
        return stack.T.astype(BF16)

    def wide(mat):
        top = high(mat)
        rest = mat - top
        upper = jnp.concatenate([top, top], axis=1)
        lower = jnp.concatenate([rest, jnp.zeros_like(rest)], axis=1)
        return jnp.concatenate([upper, lower], axis=0).astype(BF16)

    enter = ordered(enter_t)
    enter_rows[...] = tall(enter)
    leave_rows[...] = tall(ordered(leave))
    middle_wide[...] = wide(middle[...])
    middle_t_wide[...] = wide(middle[...].T)
    scaled = enter * (1.0 / SHRINK)
    enter_t_wide[...] = wide(jnp.concatenate([scaled, jnp.zeros((8, HID), F32)], axis=0))


def offset_by(odd, low, high_):
    first = pl.multiple_of(jnp.where(odd, low, high_), 8)
    second = pl.multiple_of(jnp.where(odd, high_, low), 8)
    return first, second


def prepare_kernel(sx, sy, *refs):
    sources, (field, state, to_first, to_second), refs = refs[:3], refs[4:8], (refs[3], *refs[8:])
    odd, gradient, steady, links, sems = refs
    odd = odd[0] == 1
    copies = [
        pltpu.make_async_copy(source, target, sems.at[i])
        for i, (source, target) in enumerate(zip(sources, (gradient, steady, links)))
    ]
    for copy in copies:
        copy.start()
    blank = jnp.zeros((8, 128), F32)
    for x in range(sx):
        for y in range(sy):
            at = (x * sy + y) * ROWS + 16
            field[pl.ds(at, 8), :] = blank
            state[pl.ds(at, 8), :] = blank
    copies[0].wait()
    for x in range(sx):
        for row, k in enumerate(ORDER):
            field[pl.ds(x * sy * ROWS + row, sy, stride=ROWS), :] = gradient[k, x]
    copies[1].wait()
    copies[2].wait()
    for x in range(sx):
        for row, k in enumerate(ORDER):
            state[pl.ds(x * sy * ROWS + row, sy, stride=ROWS), :] = steady[k, x]
        for word in range(2):
            state[pl.ds(x * sy * ROWS + Q + word, sy, stride=ROWS), :] = links[word, x].astype(F32)
    at = 0
    for ref, depth in ((field, 3), (state, 2)):
        for x in range(sx):
            size = depth * ROWS
            first, second = offset_by(odd, x * sy * ROWS, (x * sy + sy - depth) * ROWS)
            to_first[pl.ds(at, size), :] = ref[pl.ds(first, size), :]
            to_second[pl.ds(at, size), :] = ref[pl.ds(second, size), :]
            at += size


def sublane():
    return lax.broadcasted_iota(jnp.int32, (8, 128), 0)


def row_constants(values):
    row = sublane()
    out = jnp.zeros((8, 128), jnp.int32)
    for at, value in enumerate(values):
        out = jnp.where(row == at, value, out)
    return out


def codes_of(tail):
    word_0 = jnp.broadcast_to(tail[3:4, :].astype(jnp.int32), (8, 128))
    word_1 = jnp.broadcast_to(tail[4:5, :].astype(jnp.int32), (8, 128))
    solid = (word_1 & (1 << (18 - 10))) != 0
    codes = []
    for group in range(3):
        members = [ORDER[group * 8 + i] if group * 8 + i < Q else -1 for i in range(8)]
        second = row_constants([1 if k >= 10 else 0 for k in members])
        bit = row_constants([0 if k < 0 else 1 << (k % 10) for k in members])
        pad = row_constants([1 if k < 0 else 0 for k in members])
        word = jnp.where(second == 1, word_1, word_0)
        code = jnp.where((word & bit) != 0, 1.0, 0.0)
        codes.append(jnp.where(jnp.logical_or(solid, pad == 1), 2.0, code))
    return codes


def slopes_of(columns, enter_rows, middle_wide, slope_one, slope_two, codes):
    enter = enter_rows[:, 0:80]
    middle = middle_wide[...]

    def chunk(at):
        pair = [ref[pl.ds(offset, ROWS), :] for ref, offset in columns[at : at + 2]]
        hidden = jnp.tanh(rows_dot(enter, jnp.concatenate(pair, axis=1)))
        yield True
        one = 1.0 - hidden * hidden
        hidden = jnp.tanh(wide_dot(middle, hidden))
        yield True
        two = 1.0 - hidden * hidden
        for i in range(2):
            slope_one[at + i] = one[:, i * 128 : (i + 1) * 128]
            slope_two[at + i] = two[:, i * 128 : (i + 1) * 128]
            for group, code in enumerate(codes_of(pair[i][16:24, :])):
                codes[at + i, group * 8 : group * 8 + 8, :] = code

    together(chunk(at) for at in range(0, len(columns), 2))


def own_slopes_kernel(count, state, enter_rows, middle_wide, slope_one, slope_two, codes):
    columns = [(state, i * ROWS) for i in range(count)]
    slopes_of(columns, enter_rows, middle_wide, slope_one, slope_two, codes)


def halo_slopes_kernel(sx, low, high_, enter_rows, middle_wide, slope_one, slope_two, codes):
    columns = []
    for x in range(sx):
        for ref in (low, high_):
            for row in range(2):
                columns.append((ref, (sx * 3 + x * 2 + row) * ROWS))
    slopes_of(columns, enter_rows, middle_wide, slope_one, slope_two, codes)


def face_shape(height, sz):
    return (-(-(height * FACE + 8 - FACE) // 8) * 8, sz)


def face(out, at, rows):
    out[pl.ds(at * FACE, FACE), :] = rows[0:FACE]


def face_tail(height, *outs):
    for out in outs:
        used = height * FACE
        out[pl.ds(used, out.shape[0] - used), :] = jnp.zeros((out.shape[0] - used, out.shape[1]), F32)


def faces_kernel(sx, sy, odd_x, odd_y, field, first, second, _, low, high_, to_first, to_second):
    odd = jnp.full((8, 128), odd_y[0]) == 1
    for at in range(0, first.shape[0], 8):
        one, two = first[pl.ds(at, 8), :], second[pl.ds(at, 8), :]
        low[pl.ds(at, 8), :] = jnp.where(odd, one, two)
        high_[pl.ds(at, 8), :] = jnp.where(odd, two, one)
    face_tail(sy + 6, to_first, to_second)
    odd = jnp.full((8, 128), odd_x[0]) == 1
    for row in range(-3, sy + 3):
        down = column(sy, field, low, high_, 0, row, 0)
        up = column(sy, field, low, high_, sx - 1, row, 8)
        face(to_first, row + 3, jnp.where(odd, down, up))
        face(to_second, row + 3, jnp.where(odd, up, down))


def column(sy, field, low, high_, x, row, group):
    if row < 0:
        return low[pl.ds((x * 3 + row + 3) * ROWS + group, 8), :]
    if row >= sy:
        return high_[pl.ds((x * 3 + row - sy) * ROWS + group, 8), :]
    return field[pl.ds((x * sy + row) * ROWS + group, 8), :]


def pull_column(get, code, x, row):
    at = sublane()
    straight = jnp.logical_or(at == 0, jnp.logical_or(at == 3, at == 4))
    first = jnp.logical_or(at == 3, at == 6)
    second = jnp.logical_or(at == 4, at == 7)
    own = [get(x, row, group) for group in (0, 8, 16)]
    out = []
    for group, step in ((0, 1), (8, -1)):
        value = jnp.where(straight, get(x + step, row, group), get(x, row + step, group))
        value = jnp.where(at == 1, get(x + step, row + step, group), value)
        value = jnp.where(at == 2, get(x + step, row - step, group), value)
        up = pltpu.roll(value, 127, 1)
        down = pltpu.roll(value, 1, 1)
        if step < 0:
            up, down = down, up
        out.append(jnp.where(first, up, jnp.where(second, down, value)))
    up = pltpu.roll(own[2], 127, 1)
    down = pltpu.roll(own[2], 1, 1)
    out.append(jnp.where(at == 0, up, jnp.where(at == 1, down, own[2])))
    swapped = jnp.where(at == 0, pltpu.roll(own[2], 7, 0), jnp.where(at == 1, pltpu.roll(own[2], 1, 0), own[2]))
    result = []
    for pulled, back, flag in zip(out, (own[1], own[0], swapped), (code(0), code(8), code(16))):
        result.append(jnp.where(flag == 0.0, pulled, jnp.where(flag == 1.0, back, 0.0)))
    return jnp.concatenate(result, axis=0)


def apply_rows(sx, first, last, get, table, leave_rows, middle_t_wide, enter_t_wide, put):
    leave = leave_rows[:, 0:80]
    middle = middle_t_wide[...]
    enter = enter_t_wide[...]

    def chunk(x, row):
        entries = [table(x, r) for r in range(row, min(row + SPAN, last))]
        reads = [
            pull_column(get, lambda g, codes=codes, at=at: codes[at, g : g + 8, :], x, row + i)
            for i, (_, _, codes, at) in enumerate(entries)
        ]
        read = jnp.concatenate(reads, axis=1)
        yield True
        carried = rows_dot(leave, read) * jnp.concatenate([two[at] for _, two, _, at in entries], axis=1)
        yield True
        carried = wide_dot(middle, carried) * jnp.concatenate([one[at] for one, _, _, at in entries], axis=1)
        yield True
        image = (0.5 / SHRINK) * read + wide_dot(enter, carried)[:ROWS]
        for i in range(len(entries)):
            put(x, row + i, image[:, i * 128 : (i + 1) * 128])

    together(chunk(x, row) for x in range(sx) for row in range(first, last, SPAN))


def table_of(sy, refs):
    one, two, codes, one_h, two_h, codes_h = refs

    def table(x, row):
        if 0 <= row < sy:
            return one, two, codes, x * sy + row
        return one_h, two_h, codes_h, x * 4 + (row + 2 if row < 0 else row - sy + 2)

    return table


def apply_kernel(sx, sy, step, *refs):
    odd_x, *refs = refs
    odd = jnp.full((8, 128), odd_x[0]) == 1
    if step == 1:
        field, low, high_ = refs[:3]
        refs = refs[3:]

        def inner(x, row, group):
            return column(sy, field, low, high_, x, row, group)

    else:
        previous = refs[0]
        refs = refs[1:]
        depth = 4 - step
        height = sy + 2 * depth

        def inner(x, row, group):
            return previous[pl.ds((x * height + row + depth) * ROWS + group, 8), :]

    first, second = refs[:2]
    table = table_of(sy, refs[2:8])
    leave_rows, middle_t_wide, enter_t_wide = refs[8:11]
    refs = refs[11:]
    before = 4 - step
    seen = {}

    def beside(row):
        if row not in seen:
            one = first[pl.ds((row + before) * FACE, 8), :]
            two = second[pl.ds((row + before) * FACE, 8), :]
            seen[row] = jnp.where(odd, one, two), jnp.where(odd, two, one)
        return seen[row]

    def get(x, row, group):
        if x < 0:
            return beside(row)[0]
        if x >= sx:
            return beside(row)[1]
        return inner(x, row, group)

    after = 3 - step
    height_out = sy + 2 * after
    if step < 3:
        image, to_first, to_second = refs
        face_tail(height_out, to_first, to_second)

        def put(x, row, value):
            image[pl.ds((x * height_out + row + after) * ROWS, ROWS), :] = value

        apply_rows(sx, -after, sy + after, get, table, leave_rows, middle_t_wide, enter_t_wide, put)
        one, two = offset_by(odd_x[0] == 1, 0, (sx - 1) * height_out * ROWS + 8)
        for row in range(height_out):
            face(to_first, row, image[pl.ds(one + row * ROWS, 8), :])
            face(to_second, row, image[pl.ds(two + row * ROWS, 8), :])
        return

    field, image_one, out = refs
    totals = [jnp.zeros((8, 128), F32) for _ in range(10)]

    def put(x, row, value):
        for group in (0, 8, 16):
            parts = (
                field[pl.ds((x * sy + row) * ROWS + group, 8), :],
                image_one[pl.ds((x * (sy + 4) + row + 2) * ROWS + group, 8), :],
                inner(x, row, group),
                value[group : group + 8],
            )
            at = 0
            for i in range(4):
                for j in range(i, 4):
                    totals[at] = totals[at] + parts[i] * parts[j]
                    at += 1

    apply_rows(sx, 0, sy, get, table, leave_rows, middle_t_wide, enter_t_wide, put)
    sums = jnp.concatenate(
        [jnp.sum(total, axis=0, keepdims=True) for total in totals] + [jnp.zeros((6, 128), F32)], axis=0
    )
    sums = jnp.broadcast_to(jnp.sum(sums, axis=1, keepdims=True), (16, 128))
    place = lax.broadcasted_iota(jnp.int32, (16, 128), 0) == lax.broadcasted_iota(jnp.int32, (16, 128), 1)
    line = jnp.sum(jnp.where(place, sums, 0.0), axis=0, keepdims=True)
    for i in range(out.shape[0]):
        out[i] = line


def least_squares(hess, target):
    rows = [list(line) for line in hess]
    target = list(target)
    for col in range(ITERS):
        upper = rows[col][col]
        lower = rows[col + 1][col]
        radius = jnp.sqrt(upper * upper + lower * lower)
        cosine = upper / radius
        sine = lower / radius
        for other in range(col, ITERS):
            first_value = rows[col][other]
            second_value = rows[col + 1][other]
            rows[col][other] = cosine * first_value + sine * second_value
            rows[col + 1][other] = cosine * second_value - sine * first_value
        first_value = target[col]
        second_value = target[col + 1]
        target[col] = cosine * first_value + sine * second_value
        target[col + 1] = cosine * second_value - sine * first_value
    coeffs = [None] * ITERS
    for col in reversed(range(ITERS)):
        accum = target[col]
        for other in range(col + 1, ITERS):
            accum = accum - rows[col][other] * coeffs[other]
        coeffs[col] = accum / rows[col][col]
    return coeffs


def finish_kernel(sx, sy, parts, gradient, image_one, image_two, out):
    total = parts[0]
    for i in range(1, parts.shape[0]):
        total = total + parts[i]
    total = jnp.broadcast_to(total, (8, 128))
    lane = lax.broadcasted_iota(jnp.int32, (8, 128), 1)
    gram = [[None] * 4 for _ in range(4)]
    at = 0
    for i in range(4):
        for j in range(i, 4):
            one = jnp.sum(jnp.where(lane == at, total, 0.0), axis=1, keepdims=True)
            gram[i][j] = gram[j][i] = jnp.broadcast_to(one, (8, 128))
            at += 1
    size = [jnp.sqrt(gram[i][i]) for i in range(4)]
    inverse = [1.0 / value for value in size]
    cosines = [[gram[i][j] * inverse[i] * inverse[j] for j in range(4)] for i in range(4)]
    zero = jnp.zeros((8, 128), F32)
    one = zero + 1.0
    lower = [[zero] * 4 for _ in range(4)]
    for i in range(4):
        for j in range(i + 1):
            value = one if i == j else cosines[i][j]
            for k in range(j):
                value = value - lower[i][k] * lower[j][k]
            lower[i][j] = jnp.sqrt(jnp.maximum(value, FLOOR)) if i == j else value / lower[j][j]
    hess = [[zero] * ITERS for _ in range(ITERS + 1)]
    for j in range(ITERS):
        ratio = SHRINK * size[j + 1] * inverse[j]
        for i in range(j + 2):
            hess[i][j] = lower[j][i] - ratio * lower[j + 1][i]
    coeffs = least_squares(hess, [one, zero, zero, zero])
    scaled = [coeffs[j] * size[0] * inverse[j] for j in range(ITERS)]
    for x in range(sx):
        for row, k in enumerate(ORDER):
            second = image_one[pl.ds((x * (sy + 4) + 2) * ROWS + row, sy, stride=ROWS), :]
            third = image_two[pl.ds((x * (sy + 2) + 1) * ROWS + row, sy, stride=ROWS), :]
            out[k, x] = scaled[0] * gradient[k, x] + scaled[1] * second + scaled[2] * third


def exchange(axis, to_first, to_second):
    count = lax.axis_size(axis)
    near = [(i, i ^ 1) for i in range(count)]
    far = [(i, ((i + 1) ^ 1) - 1) for i in range(1, count - 1)]
    second = lax.ppermute(to_second, axis, far)
    first = lax.ppermute(to_first, axis, near)
    return first, second


def per_device(gradient, steady_state, enter_weight, middle_weight, leave_weight, links):
    sx, sy, sz = gradient.shape[1:]
    own = sx * sy
    odd_x, odd_y = [(lax.axis_index(axis) % 2).reshape(1) for axis in ("gx", "gy")]

    def bind(kernel, *static):
        def bound(*refs):
            kernel(*static, *refs)

        bound.__name__ = kernel.__name__
        return bound

    flat = (own * ROWS, sz)
    message = (sx * 5 * ROWS, sz)
    field, state, to_first, to_second = pl.pallas_call(
        bind(prepare_kernel, sx, sy),
        out_shape=[jax.ShapeDtypeStruct(shape, F32) for shape in (flat, flat, message, message)],
        in_specs=[pl.BlockSpec(memory_space=pltpu.HBM)] * 3 + [SM],
        out_specs=[VM] * 4,
        scratch_shapes=[pltpu.VMEM(x.shape, x.dtype) for x in (gradient, steady_state, links)]
        + [pltpu.SemaphoreType.DMA((3,))],
        compiler_params=pltpu.CompilerParams(vmem_limit_bytes=VMEM_BYTES),
    )(*[pltpu.with_memory_space_constraint(x, pltpu.HBM) for x in (gradient, steady_state, links)], odd_y)
    first, second = exchange("gy", to_first, to_second)
    enter_rows, leave_rows, middle_wide, middle_t_wide, enter_t_wide = call(
        weights_kernel,
        [((HID, HID), BF16), ((HID, HID), BF16), ((2 * HID, 2 * HID), BF16), ((2 * HID, 2 * HID), BF16), ((64, 2 * HID), BF16)],
        enter_weight.T, middle_weight, leave_weight,
    )

    def tables(count):
        return [((count, HID, sz), F32), ((count, HID, sz), F32), ((count, ROWS, sz), F32)]

    own_table = call(bind(own_slopes_kernel, own), tables(own), state, enter_rows, middle_wide)
    low, high_, to_first, to_second = call(
        bind(faces_kernel, sx, sy),
        [(message, F32)] * 2 + [(face_shape(sy + 6, sz), F32)] * 2,
        odd_x, odd_y, field, first, second, own_table[2],
    )
    first, second = exchange("gx", to_first, to_second)
    halo_table = call(
        bind(halo_slopes_kernel, sx), tables(sx * 4), low, high_, enter_rows, middle_wide
    )
    shared = (*own_table, *halo_table, leave_rows, middle_t_wide, enter_t_wide)

    def image_shapes(depth):
        height = sy + 2 * depth
        return [((sx * height * ROWS, sz), F32), (face_shape(height, sz), F32), (face_shape(height, sz), F32)]

    image_one, to_first, to_second = call(
        bind(apply_kernel, sx, sy, 1), image_shapes(2), odd_x, field, low, high_, first, second, *shared
    )
    first, second = exchange("gx", to_first, to_second)
    image_two, to_first, to_second = call(
        bind(apply_kernel, sx, sy, 2), image_shapes(1), odd_x, image_one, first, second, *shared
    )
    first, second = exchange("gx", to_first, to_second)
    count_y = lax.axis_size("gy")
    count_x = lax.axis_size("gx")

    def last_kernel(*refs):
        *refs, field, image_one, out = refs
        apply_kernel(sx, sy, 3, *refs, field, image_one, out)

    (line,) = call(
        last_kernel, [((count_y, 1, sz), F32)], odd_x, image_two, first, second, *shared, field, image_one
    )
    line = jnp.sum(lax.all_to_all(line, "gy", 0, 0), axis=0, keepdims=True)
    parts = lax.all_to_all(jnp.broadcast_to(line, (count_x, 1, sz)), "gx", 0, 0)
    (adjoint,) = call(
        bind(finish_kernel, sx, sy), [(gradient.shape, F32)], parts, gradient, image_one, image_two
    )
    return adjoint


def solution(mesh):
    in_specs = (
        P(None, "gx", "gy", None),
        P(None, "gx", "gy", None),
        P(),
        P(),
        P(),
        P(None, "gx", "gy", None),
    )
    out_specs = P(None, "gx", "gy", None)
    return jax.shard_map(
        per_device, mesh=mesh, in_specs=in_specs, out_specs=out_specs, check_vma=False
    )
```

```python
import jax
import jax.numpy as jnp
from jax import lax
from jax.experimental import pallas as pl
from jax.experimental.pallas import tpu as pltpu
from jax.sharding import PartitionSpec as P


Q = 19
HID = 128
ITERS = 3
ROWS = 24
SHRINK = 16.0
FLOOR = 1e-10
VMEM_BYTES = 16 * 1024 * 1024
SPAN = 6
FACE = 5

ORDER = (0, 4, 6, 8, 10, 2, 12, 14, 1, 5, 7, 9, 11, 3, 13, 15, 16, 17, 18)

F32 = jnp.float32
BF16 = jnp.bfloat16
VM = pl.BlockSpec(memory_space=pltpu.VMEM)
SM = pl.BlockSpec(memory_space=pltpu.SMEM)


def call(kernel, outs, *args):
    return pl.pallas_call(
        kernel,
        out_shape=[jax.ShapeDtypeStruct(shape, kind) for shape, kind in outs],
        in_specs=[SM if x.shape == (1,) else VM for x in args],
        out_specs=[VM] * len(outs),
        compiler_params=pltpu.CompilerParams(vmem_limit_bytes=VMEM_BYTES),
    )(*args)


def high(x):
    return x.astype(BF16).astype(F32)


def rows_dot(weights, x):
    top = high(x)
    stack = jnp.concatenate([top, top, x - top, jnp.zeros((8, x.shape[1]), F32)], axis=0)
    return jnp.dot(weights, stack.astype(BF16), preferred_element_type=F32)


def wide_dot(weights, x):
    top = x.astype(BF16)
    rest = (x - top.astype(F32)).astype(BF16)
    both = jnp.dot(weights, jnp.concatenate([top, rest], axis=0), preferred_element_type=F32)
    half = weights.shape[0] // 2
    return both[:half] + both[half:]


def together(chunks):
    chunks = list(chunks)
    for at in range(0, len(chunks), 4):
        running = chunks[at : at + 4]
        while running:
            running = [chunk for chunk in running if next(chunk, None)]


def weights_kernel(enter_t, middle, leave, enter_rows, leave_rows, middle_wide, middle_t_wide, enter_t_wide):
    def ordered(ref):
        rows = [ref[k : k + 1, :] for k in ORDER]
        return jnp.concatenate(rows + [jnp.zeros((ROWS - Q, HID), F32)], axis=0)

    def tall(rows):
        top = high(rows)
        stack = jnp.concatenate([top, rows - top, top, jnp.zeros((HID - 3 * ROWS, HID), F32)], axis=0)
        return stack.T.astype(BF16)

    def wide(mat):
        top = high(mat)
        rest = mat - top
        upper = jnp.concatenate([top, top], axis=1)
        lower = jnp.concatenate([rest, jnp.zeros_like(rest)], axis=1)
        return jnp.concatenate([upper, lower], axis=0).astype(BF16)

    enter = ordered(enter_t)
    enter_rows[...] = tall(enter)
    leave_rows[...] = tall(ordered(leave))
    middle_wide[...] = wide(middle[...])
    middle_t_wide[...] = wide(middle[...].T)
    scaled = enter * (1.0 / SHRINK)
    enter_t_wide[...] = wide(jnp.concatenate([scaled, jnp.zeros((8, HID), F32)], axis=0))


def offset_by(odd, low, high_):
    first = pl.multiple_of(jnp.where(odd, low, high_), 8)
    second = pl.multiple_of(jnp.where(odd, high_, low), 8)
    return first, second


def prepare_kernel(sx, sy, *refs):
    sources, odd, (field, state, to_first, to_second) = refs[:6], refs[6], refs[7:11]
    weights, (gradient, steady, links, sems) = refs[11:14], refs[14:]
    odd = odd[0] == 1
    copies = [
        pltpu.make_async_copy(source, target, sems.at[i])
        for i, (source, target) in enumerate(zip(sources, (gradient, steady, links, *weights)))
    ]
    for copy in copies:
        copy.start()
    blank = jnp.zeros((8, 128), F32)
    for x in range(sx):
        for y in range(sy):
            at = (x * sy + y) * ROWS + 16
            field[pl.ds(at, 8), :] = blank
            state[pl.ds(at, 8), :] = blank
    copies[0].wait()
    for x in range(sx):
        for row, k in enumerate(ORDER):
            field[pl.ds(x * sy * ROWS + row, sy, stride=ROWS), :] = gradient[k, x]
    copies[1].wait()
    copies[2].wait()
    for x in range(sx):
        for row, k in enumerate(ORDER):
            state[pl.ds(x * sy * ROWS + row, sy, stride=ROWS), :] = steady[k, x]
        for word in range(2):
            state[pl.ds(x * sy * ROWS + Q + word, sy, stride=ROWS), :] = links[word, x].astype(F32)
    at = 0
    for ref, depth in ((field, 3), (state, 2)):
        for x in range(sx):
            size = depth * ROWS
            first, second = offset_by(odd, x * sy * ROWS, (x * sy + sy - depth) * ROWS)
            to_first[pl.ds(at, size), :] = ref[pl.ds(first, size), :]
            to_second[pl.ds(at, size), :] = ref[pl.ds(second, size), :]
            at += size
    for copy in copies[3:]:
        copy.wait()


def sublane():
    return lax.broadcasted_iota(jnp.int32, (8, 128), 0)


def row_constants(values):
    row = sublane()
    out = jnp.zeros((8, 128), jnp.int32)
    for at, value in enumerate(values):
        out = jnp.where(row == at, value, out)
    return out


def codes_of(tail):
    word_0 = jnp.broadcast_to(tail[3:4, :].astype(jnp.int32), (8, 128))
    word_1 = jnp.broadcast_to(tail[4:5, :].astype(jnp.int32), (8, 128))
    solid = (word_1 & (1 << (18 - 10))) != 0
    codes = []
    for group in range(3):
        members = [ORDER[group * 8 + i] if group * 8 + i < Q else -1 for i in range(8)]
        second = row_constants([1 if k >= 10 else 0 for k in members])
        bit = row_constants([0 if k < 0 else 1 << (k % 10) for k in members])
        pad = row_constants([1 if k < 0 else 0 for k in members])
        word = jnp.where(second == 1, word_1, word_0)
        code = jnp.where((word & bit) != 0, 1.0, 0.0)
        codes.append(jnp.where(jnp.logical_or(solid, pad == 1), 2.0, code))
    return codes


def slopes_of(columns, enter_rows, middle_wide, slope_one, slope_two, codes):
    enter = enter_rows[:, 0:80]
    middle = middle_wide[...]

    def chunk(at):
        pair = [ref[pl.ds(offset, ROWS), :] for ref, offset in columns[at : at + 2]]
        hidden = jnp.tanh(rows_dot(enter, jnp.concatenate(pair, axis=1)))
        yield True
        one = 1.0 - hidden * hidden
        hidden = jnp.tanh(wide_dot(middle, hidden))
        yield True
        two = 1.0 - hidden * hidden
        for i in range(2):
            slope_one[at + i] = one[:, i * 128 : (i + 1) * 128]
            slope_two[at + i] = two[:, i * 128 : (i + 1) * 128]
            for group, code in enumerate(codes_of(pair[i][16:24, :])):
                codes[at + i, group * 8 : group * 8 + 8, :] = code

    together(chunk(at) for at in range(0, len(columns), 2))


def own_slopes_kernel(count, state, enter_rows, middle_wide, slope_one, slope_two, codes):
    columns = [(state, i * ROWS) for i in range(count)]
    slopes_of(columns, enter_rows, middle_wide, slope_one, slope_two, codes)


def halo_slopes_kernel(sx, low, high_, enter_rows, middle_wide, slope_one, slope_two, codes):
    columns = []
    for x in range(sx):
        for ref in (low, high_):
            for row in range(2):
                columns.append((ref, (sx * 3 + x * 2 + row) * ROWS))
    slopes_of(columns, enter_rows, middle_wide, slope_one, slope_two, codes)


def face_shape(height, sz):
    return (-(-(height * FACE + 8 - FACE) // 8) * 8, sz)


def face(out, at, rows):
    out[pl.ds(at * FACE, FACE), :] = rows[0:FACE]


def face_tail(height, *outs):
    for out in outs:
        used = height * FACE
        out[pl.ds(used, out.shape[0] - used), :] = jnp.zeros((out.shape[0] - used, out.shape[1]), F32)


def faces_kernel(sx, sy, odd_x, odd_y, field, first, second, _, low, high_, to_first, to_second):
    odd = jnp.full((8, 128), odd_y[0]) == 1
    for at in range(0, first.shape[0], 8):
        one, two = first[pl.ds(at, 8), :], second[pl.ds(at, 8), :]
        low[pl.ds(at, 8), :] = jnp.where(odd, one, two)
        high_[pl.ds(at, 8), :] = jnp.where(odd, two, one)
    face_tail(sy + 6, to_first, to_second)
    odd = jnp.full((8, 128), odd_x[0]) == 1
    for row in range(-3, sy + 3):
        down = column(sy, field, low, high_, 0, row, 0)
        up = column(sy, field, low, high_, sx - 1, row, 8)
        face(to_first, row + 3, jnp.where(odd, down, up))
        face(to_second, row + 3, jnp.where(odd, up, down))


def column(sy, field, low, high_, x, row, group):
    if row < 0:
        return low[pl.ds((x * 3 + row + 3) * ROWS + group, 8), :]
    if row >= sy:
        return high_[pl.ds((x * 3 + row - sy) * ROWS + group, 8), :]
    return field[pl.ds((x * sy + row) * ROWS + group, 8), :]


def pull_column(get, code, x, row):
    at = sublane()
    straight = jnp.logical_or(at == 0, jnp.logical_or(at == 3, at == 4))
    first = jnp.logical_or(at == 3, at == 6)
    second = jnp.logical_or(at == 4, at == 7)
    own = [get(x, row, group) for group in (0, 8, 16)]
    out = []
    for group, step in ((0, 1), (8, -1)):
        value = jnp.where(straight, get(x + step, row, group), get(x, row + step, group))
        value = jnp.where(at == 1, get(x + step, row + step, group), value)
        value = jnp.where(at == 2, get(x + step, row - step, group), value)
        up = pltpu.roll(value, 127, 1)
        down = pltpu.roll(value, 1, 1)
        if step < 0:
            up, down = down, up
        out.append(jnp.where(first, up, jnp.where(second, down, value)))
    up = pltpu.roll(own[2], 127, 1)
    down = pltpu.roll(own[2], 1, 1)
    out.append(jnp.where(at == 0, up, jnp.where(at == 1, down, own[2])))
    swapped = jnp.where(at == 0, pltpu.roll(own[2], 7, 0), jnp.where(at == 1, pltpu.roll(own[2], 1, 0), own[2]))
    result = []
    for pulled, back, flag in zip(out, (own[1], own[0], swapped), (code(0), code(8), code(16))):
        result.append(jnp.where(flag == 0.0, pulled, jnp.where(flag == 1.0, back, 0.0)))
    return jnp.concatenate(result, axis=0)


def apply_rows(sx, first, last, get, table, leave_rows, middle_t_wide, enter_t_wide, put):
    leave = leave_rows[:, 0:80]
    middle = middle_t_wide[...]
    enter = enter_t_wide[...]

    def chunk(x, row):
        entries = [table(x, r) for r in range(row, min(row + SPAN, last))]
        reads = [
            pull_column(get, lambda g, codes=codes, at=at: codes[at, g : g + 8, :], x, row + i)
            for i, (_, _, codes, at) in enumerate(entries)
        ]
        read = jnp.concatenate(reads, axis=1)
        yield True
        carried = rows_dot(leave, read) * jnp.concatenate([two[at] for _, two, _, at in entries], axis=1)
        yield True
        carried = wide_dot(middle, carried) * jnp.concatenate([one[at] for one, _, _, at in entries], axis=1)
        yield True
        image = (0.5 / SHRINK) * read + wide_dot(enter, carried)[:ROWS]
        for i in range(len(entries)):
            put(x, row + i, image[:, i * 128 : (i + 1) * 128])

    together(chunk(x, row) for x in range(sx) for row in range(first, last, SPAN))


def table_of(sy, refs):
    one, two, codes, one_h, two_h, codes_h = refs

    def table(x, row):
        if 0 <= row < sy:
            return one, two, codes, x * sy + row
        return one_h, two_h, codes_h, x * 4 + (row + 2 if row < 0 else row - sy + 2)

    return table


def apply_kernel(sx, sy, step, *refs):
    odd_x, *refs = refs
    odd = jnp.full((8, 128), odd_x[0]) == 1
    if step == 1:
        field, low, high_ = refs[:3]
        refs = refs[3:]

        def inner(x, row, group):
            return column(sy, field, low, high_, x, row, group)

    else:
        previous = refs[0]
        refs = refs[1:]
        depth = 4 - step
        height = sy + 2 * depth

        def inner(x, row, group):
            return previous[pl.ds((x * height + row + depth) * ROWS + group, 8), :]

    first, second = refs[:2]
    table = table_of(sy, refs[2:8])
    leave_rows, middle_t_wide, enter_t_wide = refs[8:11]
    refs = refs[11:]
    before = 4 - step
    seen = {}

    def beside(row):
        if row not in seen:
            one = first[pl.ds((row + before) * FACE, 8), :]
            two = second[pl.ds((row + before) * FACE, 8), :]
            seen[row] = jnp.where(odd, one, two), jnp.where(odd, two, one)
        return seen[row]

    def get(x, row, group):
        if x < 0:
            return beside(row)[0]
        if x >= sx:
            return beside(row)[1]
        return inner(x, row, group)

    after = 3 - step
    height_out = sy + 2 * after
    if step < 3:
        image, to_first, to_second = refs
        face_tail(height_out, to_first, to_second)

        def put(x, row, value):
            image[pl.ds((x * height_out + row + after) * ROWS, ROWS), :] = value

        apply_rows(sx, -after, sy + after, get, table, leave_rows, middle_t_wide, enter_t_wide, put)
        one, two = offset_by(odd_x[0] == 1, 0, (sx - 1) * height_out * ROWS + 8)
        for row in range(height_out):
            face(to_first, row, image[pl.ds(one + row * ROWS, 8), :])
            face(to_second, row, image[pl.ds(two + row * ROWS, 8), :])
        return

    field, image_one, out = refs
    totals = [jnp.zeros((8, 128), F32) for _ in range(10)]

    def put(x, row, value):
        for group in (0, 8, 16):
            parts = (
                field[pl.ds((x * sy + row) * ROWS + group, 8), :],
                image_one[pl.ds((x * (sy + 4) + row + 2) * ROWS + group, 8), :],
                inner(x, row, group),
                value[group : group + 8],
            )
            at = 0
            for i in range(4):
                for j in range(i, 4):
                    totals[at] = totals[at] + parts[i] * parts[j]
                    at += 1

    apply_rows(sx, 0, sy, get, table, leave_rows, middle_t_wide, enter_t_wide, put)
    sums = jnp.concatenate(
        [jnp.sum(total, axis=0, keepdims=True) for total in totals] + [jnp.zeros((6, 128), F32)], axis=0
    )
    sums = jnp.broadcast_to(jnp.sum(sums, axis=1, keepdims=True), (16, 128))
    place = lax.broadcasted_iota(jnp.int32, (16, 128), 0) == lax.broadcasted_iota(jnp.int32, (16, 128), 1)
    line = jnp.sum(jnp.where(place, sums, 0.0), axis=0, keepdims=True)
    for i in range(out.shape[0]):
        out[i] = line


def least_squares(hess, target):
    rows = [list(line) for line in hess]
    target = list(target)
    for col in range(ITERS):
        upper = rows[col][col]
        lower = rows[col + 1][col]
        radius = jnp.sqrt(upper * upper + lower * lower)
        cosine = upper / radius
        sine = lower / radius
        for other in range(col, ITERS):
            first_value = rows[col][other]
            second_value = rows[col + 1][other]
            rows[col][other] = cosine * first_value + sine * second_value
            rows[col + 1][other] = cosine * second_value - sine * first_value
        first_value = target[col]
        second_value = target[col + 1]
        target[col] = cosine * first_value + sine * second_value
        target[col + 1] = cosine * second_value - sine * first_value
    coeffs = [None] * ITERS
    for col in reversed(range(ITERS)):
        accum = target[col]
        for other in range(col + 1, ITERS):
            accum = accum - rows[col][other] * coeffs[other]
        coeffs[col] = accum / rows[col][col]
    return coeffs


def finish_kernel(sx, sy, parts, gradient, image_one, image_two, out):
    total = parts[0]
    for i in range(1, parts.shape[0]):
        total = total + parts[i]
    total = jnp.broadcast_to(total, (8, 128))
    lane = lax.broadcasted_iota(jnp.int32, (8, 128), 1)
    gram = [[None] * 4 for _ in range(4)]
    at = 0
    for i in range(4):
        for j in range(i, 4):
            one = jnp.sum(jnp.where(lane == at, total, 0.0), axis=1, keepdims=True)
            gram[i][j] = gram[j][i] = jnp.broadcast_to(one, (8, 128))
            at += 1
    size = [jnp.sqrt(gram[i][i]) for i in range(4)]
    inverse = [1.0 / value for value in size]
    cosines = [[gram[i][j] * inverse[i] * inverse[j] for j in range(4)] for i in range(4)]
    zero = jnp.zeros((8, 128), F32)
    one = zero + 1.0
    lower = [[zero] * 4 for _ in range(4)]
    for i in range(4):
        for j in range(i + 1):
            value = one if i == j else cosines[i][j]
            for k in range(j):
                value = value - lower[i][k] * lower[j][k]
            lower[i][j] = jnp.sqrt(jnp.maximum(value, FLOOR)) if i == j else value / lower[j][j]
    hess = [[zero] * ITERS for _ in range(ITERS + 1)]
    for j in range(ITERS):
        ratio = SHRINK * size[j + 1] * inverse[j]
        for i in range(j + 2):
            hess[i][j] = lower[j][i] - ratio * lower[j + 1][i]
    coeffs = least_squares(hess, [one, zero, zero, zero])
    scaled = [coeffs[j] * size[0] * inverse[j] for j in range(ITERS)]
    for x in range(sx):
        for row, k in enumerate(ORDER):
            second = image_one[pl.ds((x * (sy + 4) + 2) * ROWS + row, sy, stride=ROWS), :]
            third = image_two[pl.ds((x * (sy + 2) + 1) * ROWS + row, sy, stride=ROWS), :]
            out[k, x] = scaled[0] * gradient[k, x] + scaled[1] * second + scaled[2] * third


def exchange(axis, to_first, to_second):
    count = lax.axis_size(axis)
    near = [(i, i ^ 1) for i in range(count)]
    far = [(i, ((i + 1) ^ 1) - 1) for i in range(1, count - 1)]
    second = lax.ppermute(to_second, axis, far)
    first = lax.ppermute(to_first, axis, near)
    return first, second


def per_device(gradient, steady_state, enter_weight, middle_weight, leave_weight, links):
    sx, sy, sz = gradient.shape[1:]
    own = sx * sy
    odd_x, odd_y = [(lax.axis_index(axis) % 2).reshape(1) for axis in ("gx", "gy")]

    def bind(kernel, *static):
        def bound(*refs):
            kernel(*static, *refs)

        bound.__name__ = kernel.__name__
        return bound

    flat = (own * ROWS, sz)
    message = (sx * 5 * ROWS, sz)
    fetched = (gradient, steady_state, links, enter_weight.T, middle_weight, leave_weight)
    field, state, to_first, to_second, *fetched_weights = pl.pallas_call(
        bind(prepare_kernel, sx, sy),
        out_shape=[jax.ShapeDtypeStruct(shape, F32) for shape in (flat, flat, message, message)]
        + [jax.ShapeDtypeStruct(x.shape, x.dtype) for x in fetched[3:]],
        in_specs=[pl.BlockSpec(memory_space=pltpu.HBM)] * 6 + [SM],
        out_specs=[VM] * 7,
        scratch_shapes=[pltpu.VMEM(x.shape, x.dtype) for x in (gradient, steady_state, links)]
        + [pltpu.SemaphoreType.DMA((6,))],
        compiler_params=pltpu.CompilerParams(vmem_limit_bytes=VMEM_BYTES),
    )(*[pltpu.with_memory_space_constraint(x, pltpu.HBM) for x in fetched], odd_y)
    first, second = exchange("gy", to_first, to_second)
    enter_rows, leave_rows, middle_wide, middle_t_wide, enter_t_wide = call(
        weights_kernel,
        [((HID, HID), BF16), ((HID, HID), BF16), ((2 * HID, 2 * HID), BF16), ((2 * HID, 2 * HID), BF16), ((64, 2 * HID), BF16)],
        *fetched_weights,
    )

    def tables(count):
        return [((count, HID, sz), F32), ((count, HID, sz), F32), ((count, ROWS, sz), F32)]

    own_table = call(bind(own_slopes_kernel, own), tables(own), state, enter_rows, middle_wide)
    low, high_, to_first, to_second = call(
        bind(faces_kernel, sx, sy),
        [(message, F32)] * 2 + [(face_shape(sy + 6, sz), F32)] * 2,
        odd_x, odd_y, field, first, second, own_table[2],
    )
    first, second = exchange("gx", to_first, to_second)
    halo_table = call(
        bind(halo_slopes_kernel, sx), tables(sx * 4), low, high_, enter_rows, middle_wide
    )
    shared = (*own_table, *halo_table, leave_rows, middle_t_wide, enter_t_wide)

    def image_shapes(depth):
        height = sy + 2 * depth
        return [((sx * height * ROWS, sz), F32), (face_shape(height, sz), F32), (face_shape(height, sz), F32)]

    image_one, to_first, to_second = call(
        bind(apply_kernel, sx, sy, 1), image_shapes(2), odd_x, field, low, high_, first, second, *shared
    )
    first, second = exchange("gx", to_first, to_second)
    image_two, to_first, to_second = call(
        bind(apply_kernel, sx, sy, 2), image_shapes(1), odd_x, image_one, first, second, *shared
    )
    first, second = exchange("gx", to_first, to_second)
    count_y = lax.axis_size("gy")
    count_x = lax.axis_size("gx")

    def last_kernel(*refs):
        *refs, field, image_one, out = refs
        apply_kernel(sx, sy, 3, *refs, field, image_one, out)

    (line,) = call(
        last_kernel, [((count_y, 1, sz), F32)], odd_x, image_two, first, second, *shared, field, image_one
    )
    line = jnp.sum(lax.all_to_all(line, "gy", 0, 0), axis=0, keepdims=True)
    parts = lax.all_to_all(jnp.broadcast_to(line, (count_x, 1, sz)), "gx", 0, 0)
    (adjoint,) = call(
        bind(finish_kernel, sx, sy), [(gradient.shape, F32)], parts, gradient, image_one, image_two
    )
    return adjoint


def solution(mesh):
    in_specs = (
        P(None, "gx", "gy", None),
        P(None, "gx", "gy", None),
        P(),
        P(),
        P(),
        P(None, "gx", "gy", None),
    )
    out_specs = P(None, "gx", "gy", None)
    return jax.shard_map(
        per_device, mesh=mesh, in_specs=in_specs, out_specs=out_specs, check_vma=False
    )
```

```python
import jax
import jax.numpy as jnp
from jax import lax
from jax.experimental import pallas as pl
from jax.experimental.pallas import tpu as pltpu
from jax.sharding import PartitionSpec as P


Q = 19
HID = 128
ITERS = 3
ROWS = 24
SHRINK = 16.0
FLOOR = 1e-10
VMEM_BYTES = 16 * 1024 * 1024
SPANS = (6, 6, 6)
FACE = 5

ORDER = (0, 4, 6, 8, 10, 2, 12, 14, 1, 5, 7, 9, 11, 3, 13, 15, 16, 17, 18)

F32 = jnp.float32
BF16 = jnp.bfloat16
VM = pl.BlockSpec(memory_space=pltpu.VMEM)
SM = pl.BlockSpec(memory_space=pltpu.SMEM)


def call(kernel, outs, *args):
    return pl.pallas_call(
        kernel,
        out_shape=[jax.ShapeDtypeStruct(shape, kind) for shape, kind in outs],
        in_specs=[SM if x.shape == (1,) else VM for x in args],
        out_specs=[VM] * len(outs),
        compiler_params=pltpu.CompilerParams(vmem_limit_bytes=VMEM_BYTES),
    )(*args)


def high(x):
    return x.astype(BF16).astype(F32)


def rows_dot(weights, x):
    top = high(x)
    stack = jnp.concatenate([top, top, x - top, jnp.zeros((8, x.shape[1]), F32)], axis=0)
    return jnp.dot(weights, stack.astype(BF16), preferred_element_type=F32)


def wide_dot(weights, x):
    top = x.astype(BF16)
    rest = (x - top.astype(F32)).astype(BF16)
    both = jnp.dot(weights, jnp.concatenate([top, rest], axis=0), preferred_element_type=F32)
    half = weights.shape[0] // 2
    return both[:half] + both[half:]


def together(chunks):
    chunks = list(chunks)
    for at in range(0, len(chunks), 4):
        running = chunks[at : at + 4]
        while running:
            running = [chunk for chunk in running if next(chunk, None)]


def weights_kernel(enter_t, middle, leave, enter_rows, leave_rows, middle_wide, middle_t_wide, enter_t_wide):
    def ordered(ref):
        rows = [ref[k : k + 1, :] for k in ORDER]
        return jnp.concatenate(rows + [jnp.zeros((ROWS - Q, HID), F32)], axis=0)

    def tall(rows):
        top = high(rows)
        stack = jnp.concatenate([top, rows - top, top, jnp.zeros((HID - 3 * ROWS, HID), F32)], axis=0)
        return stack.T.astype(BF16)

    def wide(mat):
        top = high(mat)
        rest = mat - top
        upper = jnp.concatenate([top, top], axis=1)
        lower = jnp.concatenate([rest, jnp.zeros_like(rest)], axis=1)
        return jnp.concatenate([upper, lower], axis=0).astype(BF16)

    enter = ordered(enter_t)
    enter_rows[...] = tall(enter)
    leave_rows[...] = tall(ordered(leave))
    middle_wide[...] = wide(middle[...])
    middle_t_wide[...] = wide(middle[...].T)
    scaled = enter * (1.0 / SHRINK)
    enter_t_wide[...] = wide(jnp.concatenate([scaled, jnp.zeros((8, HID), F32)], axis=0))


def offset_by(odd, low, high_):
    first = pl.multiple_of(jnp.where(odd, low, high_), 8)
    second = pl.multiple_of(jnp.where(odd, high_, low), 8)
    return first, second


def prepare_kernel(sx, sy, *refs):
    sources, odd, (field, state, to_first, to_second) = refs[:6], refs[6], refs[7:11]
    weights, (gradient, steady, links, sems) = refs[11:14], refs[14:]
    odd = odd[0] == 1
    copies = [
        pltpu.make_async_copy(source, target, sems.at[i])
        for i, (source, target) in enumerate(zip(sources, (gradient, steady, links, *weights)))
    ]
    for copy in copies:
        copy.start()
    blank = jnp.zeros((8, 128), F32)
    for x in range(sx):
        for y in range(sy):
            at = (x * sy + y) * ROWS + 16
            field[pl.ds(at, 8), :] = blank
            state[pl.ds(at, 8), :] = blank
    copies[0].wait()
    for x in range(sx):
        for row, k in enumerate(ORDER):
            field[pl.ds(x * sy * ROWS + row, sy, stride=ROWS), :] = gradient[k, x]
    copies[1].wait()
    copies[2].wait()
    for x in range(sx):
        for row, k in enumerate(ORDER):
            state[pl.ds(x * sy * ROWS + row, sy, stride=ROWS), :] = steady[k, x]
        for word in range(2):
            state[pl.ds(x * sy * ROWS + Q + word, sy, stride=ROWS), :] = links[word, x].astype(F32)
    at = 0
    for ref, depth in ((field, 3), (state, 2)):
        for x in range(sx):
            size = depth * ROWS
            first, second = offset_by(odd, x * sy * ROWS, (x * sy + sy - depth) * ROWS)
            to_first[pl.ds(at, size), :] = ref[pl.ds(first, size), :]
            to_second[pl.ds(at, size), :] = ref[pl.ds(second, size), :]
            at += size
    for copy in copies[3:]:
        copy.wait()


def sublane():
    return lax.broadcasted_iota(jnp.int32, (8, 128), 0)


def row_constants(values):
    row = sublane()
    out = jnp.zeros((8, 128), jnp.int32)
    for at, value in enumerate(values):
        out = jnp.where(row == at, value, out)
    return out


def codes_of(tail):
    word_0 = jnp.broadcast_to(tail[3:4, :].astype(jnp.int32), (8, 128))
    word_1 = jnp.broadcast_to(tail[4:5, :].astype(jnp.int32), (8, 128))
    solid = (word_1 & (1 << (18 - 10))) != 0
    codes = []
    for group in range(3):
        members = [ORDER[group * 8 + i] if group * 8 + i < Q else -1 for i in range(8)]
        second = row_constants([1 if k >= 10 else 0 for k in members])
        bit = row_constants([0 if k < 0 else 1 << (k % 10) for k in members])
        pad = row_constants([1 if k < 0 else 0 for k in members])
        word = jnp.where(second == 1, word_1, word_0)
        code = jnp.where((word & bit) != 0, 1.0, 0.0)
        codes.append(jnp.where(jnp.logical_or(solid, pad == 1), 2.0, code))
    return codes


def slopes_of(columns, enter_rows, middle_wide, slope_one, slope_two, codes):
    enter = enter_rows[:, 0:80]
    middle = middle_wide[...]

    def chunk(at):
        pair = [load() for load in columns[at : at + 2]]
        hidden = jnp.tanh(rows_dot(enter, jnp.concatenate(pair, axis=1)))
        yield True
        one = 1.0 - hidden * hidden
        hidden = jnp.tanh(wide_dot(middle, hidden))
        yield True
        two = 1.0 - hidden * hidden
        for i in range(2):
            slope_one[at + i] = one[:, i * 128 : (i + 1) * 128]
            slope_two[at + i] = two[:, i * 128 : (i + 1) * 128]
            for group, code in enumerate(codes_of(pair[i][16:24, :])):
                codes[at + i, group * 8 : group * 8 + 8, :] = code

    together(chunk(at) for at in range(0, len(columns), 2))


def loader(ref, offset):
    return lambda: ref[pl.ds(offset, ROWS), :]


def own_slopes_kernel(count, state, enter_rows, middle_wide, slope_one, slope_two, codes):
    columns = [loader(state, i * ROWS) for i in range(count)]
    slopes_of(columns, enter_rows, middle_wide, slope_one, slope_two, codes)


def halo_slopes_kernel(sx, low, high_, enter_rows, middle_wide, slope_one, slope_two, codes):
    columns = []
    for x in range(sx):
        for ref in (low, high_):
            for row in range(2):
                columns.append(loader(ref, (sx * 3 + x * 2 + row) * ROWS))
    slopes_of(columns, enter_rows, middle_wide, slope_one, slope_two, codes)


def side_slopes_kernel(sy, odd_x, first, second, enter_rows, middle_wide, slope_one, slope_two, codes):
    odd = jnp.full((ROWS, 128), odd_x[0]) == 1
    base = face_rows(sy + 6)

    def side(one, two, row):
        at = pl.ds(base + row * ROWS, ROWS)
        return lambda: jnp.where(odd, one[at, :], two[at, :])

    columns = [side(first, second, row) for row in range(sy + 2)]
    columns += [side(second, first, row) for row in range(sy + 2)]
    slopes_of(columns, enter_rows, middle_wide, slope_one, slope_two, codes)


def face_rows(height):
    return -(-(height * FACE + 8 - FACE) // 8) * 8


def face(out, base, at, rows):
    out[pl.ds(base + at * FACE, FACE), :] = rows[0:FACE]


def face_tail(base, height, *outs):
    used, size = height * FACE, face_rows(height)
    for out in outs:
        out[pl.ds(base + used, size - used), :] = jnp.zeros((size - used, out.shape[1]), F32)


def faces_kernel(sx, sy, odd_x, odd_y, field, state, first, second, _, low, high_, to_first, to_second):
    odd = jnp.full((8, 128), odd_y[0]) == 1
    for at in range(0, first.shape[0], 8):
        one, two = first[pl.ds(at, 8), :], second[pl.ds(at, 8), :]
        low[pl.ds(at, 8), :] = jnp.where(odd, one, two)
        high_[pl.ds(at, 8), :] = jnp.where(odd, two, one)
    face_tail(0, sy + 6, to_first, to_second)
    odd = jnp.full((8, 128), odd_x[0]) == 1
    for row in range(-3, sy + 3):
        down = column(sy, field, low, high_, 0, row, 0)
        up = column(sy, field, low, high_, sx - 1, row, 8)
        face(to_first, 0, row + 3, jnp.where(odd, down, up))
        face(to_second, 0, row + 3, jnp.where(odd, up, down))

    def state_column(x, row, group):
        if row < 0:
            return low[pl.ds((sx * 3 + x * 2 + row + 2) * ROWS + group, 8), :]
        if row >= sy:
            return high_[pl.ds((sx * 3 + x * 2 + row - sy) * ROWS + group, 8), :]
        return state[pl.ds((x * sy + row) * ROWS + group, 8), :]

    for row in range(-1, sy + 1):
        for group in (0, 8, 16):
            down, up = state_column(0, row, group), state_column(sx - 1, row, group)
            at = face_rows(sy + 6) + (row + 1) * ROWS + group
            to_first[pl.ds(at, 8), :] = jnp.where(odd, down, up)
            to_second[pl.ds(at, 8), :] = jnp.where(odd, up, down)


def column(sy, field, low, high_, x, row, group):
    if row < 0:
        return low[pl.ds((x * 3 + row + 3) * ROWS + group, 8), :]
    if row >= sy:
        return high_[pl.ds((x * 3 + row - sy) * ROWS + group, 8), :]
    return field[pl.ds((x * sy + row) * ROWS + group, 8), :]


def pull_column(get, code, x, row):
    at = sublane()
    straight = jnp.logical_or(at == 0, jnp.logical_or(at == 3, at == 4))
    first = jnp.logical_or(at == 3, at == 6)
    second = jnp.logical_or(at == 4, at == 7)
    own = [get(x, row, group) for group in (0, 8, 16)]
    out = []
    for group, step in ((0, 1), (8, -1)):
        value = jnp.where(straight, get(x + step, row, group), get(x, row + step, group))
        value = jnp.where(at == 1, get(x + step, row + step, group), value)
        value = jnp.where(at == 2, get(x + step, row - step, group), value)
        up = pltpu.roll(value, 127, 1)
        down = pltpu.roll(value, 1, 1)
        if step < 0:
            up, down = down, up
        out.append(jnp.where(first, up, jnp.where(second, down, value)))
    up = pltpu.roll(own[2], 127, 1)
    down = pltpu.roll(own[2], 1, 1)
    out.append(jnp.where(at == 0, up, jnp.where(at == 1, down, own[2])))
    swapped = jnp.where(at == 0, pltpu.roll(own[2], 7, 0), jnp.where(at == 1, pltpu.roll(own[2], 1, 0), own[2]))
    result = []
    for pulled, back, flag in zip(out, (own[1], own[0], swapped), (code(0), code(8), code(16))):
        result.append(jnp.where(flag == 0.0, pulled, jnp.where(flag == 1.0, back, 0.0)))
    return jnp.concatenate(result, axis=0)


def apply_rows(xs, first, last, get, table, weights, put, span):
    leave, middle, enter = weights[0][:, 0:80], weights[1][...], weights[2][...]

    def chunk(x, row):
        entries = [table(x, r) for r in range(row, min(row + span, last))]
        reads = [
            pull_column(get, lambda g, codes=codes, at=at: codes[at, g : g + 8, :], x, row + i)
            for i, (_, _, codes, at) in enumerate(entries)
        ]
        read = jnp.concatenate(reads, axis=1)
        yield True
        carried = rows_dot(leave, read) * jnp.concatenate([two[at] for _, two, _, at in entries], axis=1)
        yield True
        carried = wide_dot(middle, carried) * jnp.concatenate([one[at] for one, _, _, at in entries], axis=1)
        yield True
        image = (0.5 / SHRINK) * read + wide_dot(enter, carried)[:ROWS]
        for i in range(len(entries)):
            put(x, row + i, image[:, i * 128 : (i + 1) * 128])

    together(chunk(x, row) for x in xs for row in range(first, last, span))


def table_of(sx, sy, refs, side=None):
    one, two, codes, one_h, two_h, codes_h = refs

    def table(x, row):
        if not 0 <= x < sx:
            return *side, (row + 1 if x < 0 else sy + 2 + row + 1)
        if 0 <= row < sy:
            return one, two, codes, x * sy + row
        return one_h, two_h, codes_h, x * 4 + (row + 2 if row < 0 else row - sy + 2)

    return table


def sorted_loads(odd, first, second):
    seen = {}

    def get(at):
        if at not in seen:
            one, two = first[pl.ds(at, 8), :], second[pl.ds(at, 8), :]
            seen[at] = jnp.where(odd, one, two), jnp.where(odd, two, one)
        return seen[at]

    return get


def first_kernel(sx, sy, odd_x, field, low, high_, first, second, *refs):
    tables, weights, (image, to_first, to_second) = refs[:6], refs[6:9], refs[9:]
    beside = sorted_loads(jnp.full((8, 128), odd_x[0]) == 1, first, second)
    height = sy + 4

    def get(x, row, group):
        if x < 0:
            return beside((row + 3) * FACE)[0]
        if x >= sx:
            return beside((row + 3) * FACE)[1]
        return column(sy, field, low, high_, x, row, group)

    def put(x, row, value):
        image[pl.ds((x * height + row + 2) * ROWS, ROWS), :] = value

    near = height * ROWS
    face_tail(near, height, to_first, to_second)
    apply_rows(range(sx), -2, sy + 2, get, table_of(sx, sy, tables), weights, put, SPANS[0])
    odd = odd_x[0] == 1
    columns = offset_by(odd, 0, (sx - 1) * near)
    faces = offset_by(odd, near, (sx - 2) * near + 8)
    for out, at, face_at in zip((to_first, to_second), columns, faces):
        out[pl.ds(0, near), :] = image[pl.ds(at, near), :]
        for row in range(height):
            face(out, near, row, image[pl.ds(face_at + row * ROWS, 8), :])


def second_kernel(sx, sy, odd_x, previous, first, second, *refs):
    tables, side, weights, image = refs[:6], refs[6:9], refs[9:12], refs[12]
    beside = sorted_loads(jnp.full((8, 128), odd_x[0]) == 1, first, second)
    height = sy + 4

    def get(x, row, group):
        if 0 <= x < sx:
            return previous[pl.ds((x * height + row + 2) * ROWS + group, 8), :]
        if x in (-1, sx):
            return beside((row + 2) * ROWS + group)[0 if x < 0 else 1]
        return beside(height * ROWS + (row + 2) * FACE)[0 if x < 0 else 1]

    def put(x, row, value):
        image[pl.ds(((x + 1) * (sy + 2) + row + 1) * ROWS, ROWS), :] = value

    apply_rows(range(-1, sx + 1), -1, sy + 1, get, table_of(sx, sy, tables, side), weights, put, SPANS[1])


def third_kernel(sx, sy, previous, *refs):
    tables, weights, (field, image_one, out) = refs[:6], refs[6:9], refs[9:]

    def get(x, row, group):
        return previous[pl.ds(((x + 1) * (sy + 2) + row + 1) * ROWS + group, 8), :]

    totals = [jnp.zeros((8, 128), F32) for _ in range(10)]

    def put(x, row, value):
        for group in (0, 8, 16):
            parts = (
                field[pl.ds((x * sy + row) * ROWS + group, 8), :],
                image_one[pl.ds((x * (sy + 4) + row + 2) * ROWS + group, 8), :],
                get(x, row, group),
                value[group : group + 8],
            )
            at = 0
            for i in range(4):
                for j in range(i, 4):
                    totals[at] = totals[at] + parts[i] * parts[j]
                    at += 1

    apply_rows(range(sx), 0, sy, get, table_of(sx, sy, tables), weights, put, SPANS[2])
    sums = jnp.concatenate(
        [jnp.sum(total, axis=0, keepdims=True) for total in totals] + [jnp.zeros((6, 128), F32)], axis=0
    )
    sums = jnp.broadcast_to(jnp.sum(sums, axis=1, keepdims=True), (16, 128))
    place = lax.broadcasted_iota(jnp.int32, (16, 128), 0) == lax.broadcasted_iota(jnp.int32, (16, 128), 1)
    line = jnp.sum(jnp.where(place, sums, 0.0), axis=0, keepdims=True)
    for i in range(out.shape[0]):
        out[i] = line


def least_squares(hess, target):
    rows = [list(line) for line in hess]
    target = list(target)
    for col in range(ITERS):
        upper = rows[col][col]
        lower = rows[col + 1][col]
        radius = jnp.sqrt(upper * upper + lower * lower)
        cosine = upper / radius
        sine = lower / radius
        for other in range(col, ITERS):
            first_value = rows[col][other]
            second_value = rows[col + 1][other]
            rows[col][other] = cosine * first_value + sine * second_value
            rows[col + 1][other] = cosine * second_value - sine * first_value
        first_value = target[col]
        second_value = target[col + 1]
        target[col] = cosine * first_value + sine * second_value
        target[col + 1] = cosine * second_value - sine * first_value
    coeffs = [None] * ITERS
    for col in reversed(range(ITERS)):
        accum = target[col]
        for other in range(col + 1, ITERS):
            accum = accum - rows[col][other] * coeffs[other]
        coeffs[col] = accum / rows[col][col]
    return coeffs


def finish_kernel(sx, sy, parts, gradient, image_one, image_two, out):
    total = parts[0]
    for i in range(1, parts.shape[0]):
        total = total + parts[i]
    total = jnp.broadcast_to(total, (8, 128))
    lane = lax.broadcasted_iota(jnp.int32, (8, 128), 1)
    gram = [[None] * 4 for _ in range(4)]
    at = 0
    for i in range(4):
        for j in range(i, 4):
            one = jnp.sum(jnp.where(lane == at, total, 0.0), axis=1, keepdims=True)
            gram[i][j] = gram[j][i] = jnp.broadcast_to(one, (8, 128))
            at += 1
    size = [jnp.sqrt(gram[i][i]) for i in range(4)]
    inverse = [1.0 / value for value in size]
    cosines = [[gram[i][j] * inverse[i] * inverse[j] for j in range(4)] for i in range(4)]
    zero = jnp.zeros((8, 128), F32)
    one = zero + 1.0
    lower = [[zero] * 4 for _ in range(4)]
    for i in range(4):
        for j in range(i + 1):
            value = one if i == j else cosines[i][j]
            for k in range(j):
                value = value - lower[i][k] * lower[j][k]
            lower[i][j] = jnp.sqrt(jnp.maximum(value, FLOOR)) if i == j else value / lower[j][j]
    hess = [[zero] * ITERS for _ in range(ITERS + 1)]
    for j in range(ITERS):
        ratio = SHRINK * size[j + 1] * inverse[j]
        for i in range(j + 2):
            hess[i][j] = lower[j][i] - ratio * lower[j + 1][i]
    coeffs = least_squares(hess, [one, zero, zero, zero])
    scaled = [coeffs[j] * size[0] * inverse[j] for j in range(ITERS)]
    for x in range(sx):
        for row, k in enumerate(ORDER):
            second = image_one[pl.ds((x * (sy + 4) + 2) * ROWS + row, sy, stride=ROWS), :]
            third = image_two[pl.ds(((x + 1) * (sy + 2) + 1) * ROWS + row, sy, stride=ROWS), :]
            out[k, x] = scaled[0] * gradient[k, x] + scaled[1] * second + scaled[2] * third


def exchange(axis, to_first, to_second):
    count = lax.axis_size(axis)
    near = [(i, i ^ 1) for i in range(count)]
    far = [(i, ((i + 1) ^ 1) - 1) for i in range(1, count - 1)]
    second = lax.ppermute(to_second, axis, far)
    first = lax.ppermute(to_first, axis, near)
    return first, second


def per_device(gradient, steady_state, enter_weight, middle_weight, leave_weight, links):
    sx, sy, sz = gradient.shape[1:]
    own = sx * sy
    odd_x, odd_y = [(lax.axis_index(axis) % 2).reshape(1) for axis in ("gx", "gy")]

    def bind(kernel, *static):
        def bound(*refs):
            kernel(*static, *refs)

        bound.__name__ = kernel.__name__
        return bound

    flat = (own * ROWS, sz)
    message = (sx * 5 * ROWS, sz)
    fetched = (gradient, steady_state, links, enter_weight.T, middle_weight, leave_weight)
    field, state, to_first, to_second, *fetched_weights = pl.pallas_call(
        bind(prepare_kernel, sx, sy),
        out_shape=[jax.ShapeDtypeStruct(shape, F32) for shape in (flat, flat, message, message)]
        + [jax.ShapeDtypeStruct(x.shape, x.dtype) for x in fetched[3:]],
        in_specs=[pl.BlockSpec(memory_space=pltpu.HBM)] * 6 + [SM],
        out_specs=[VM] * 7,
        scratch_shapes=[pltpu.VMEM(x.shape, x.dtype) for x in (gradient, steady_state, links)]
        + [pltpu.SemaphoreType.DMA((6,))],
        compiler_params=pltpu.CompilerParams(vmem_limit_bytes=VMEM_BYTES),
    )(*[pltpu.with_memory_space_constraint(x, pltpu.HBM) for x in fetched], odd_y)
    first, second = exchange("gy", to_first, to_second)
    enter_rows, leave_rows, middle_wide, middle_t_wide, enter_t_wide = call(
        weights_kernel,
        [((HID, HID), BF16), ((HID, HID), BF16), ((2 * HID, 2 * HID), BF16), ((2 * HID, 2 * HID), BF16), ((64, 2 * HID), BF16)],
        *fetched_weights,
    )

    def tables(count):
        return [((count, HID, sz), F32), ((count, HID, sz), F32), ((count, ROWS, sz), F32)]

    own_table = call(bind(own_slopes_kernel, own), tables(own), state, enter_rows, middle_wide)
    low, high_, to_first, to_second = call(
        bind(faces_kernel, sx, sy),
        [(message, F32)] * 2 + [((face_rows(sy + 6) + (sy + 2) * ROWS, sz), F32)] * 2,
        odd_x, odd_y, field, state, first, second, own_table[2],
    )
    first, second = exchange("gx", to_first, to_second)
    halo_table = call(
        bind(halo_slopes_kernel, sx), tables(sx * 4), low, high_, enter_rows, middle_wide
    )
    tables_here, weights = (*own_table, *halo_table), (leave_rows, middle_t_wide, enter_t_wide)
    height = sy + 4
    side_message = (height * ROWS + face_rows(height), sz)
    image_one, to_first, to_second = call(
        bind(first_kernel, sx, sy),
        [((sx * height * ROWS, sz), F32), (side_message, F32), (side_message, F32)],
        odd_x, field, low, high_, first, second, *tables_here, *weights,
    )
    side_table = call(
        bind(side_slopes_kernel, sy), tables(2 * (sy + 2)), odd_x, first, second, enter_rows, middle_wide
    )
    first, second = exchange("gx", to_first, to_second)
    (image_two,) = call(
        bind(second_kernel, sx, sy),
        [(((sx + 2) * (sy + 2) * ROWS, sz), F32)],
        odd_x, image_one, first, second, *tables_here, *side_table, *weights,
    )
    count_y = lax.axis_size("gy")
    count_x = lax.axis_size("gx")

    (line,) = call(
        bind(third_kernel, sx, sy),
        [((count_y, 1, sz), F32)],
        image_two, *tables_here, *weights, field, image_one,
    )
    line = jnp.sum(lax.all_to_all(line, "gy", 0, 0), axis=0, keepdims=True)
    parts = lax.all_to_all(jnp.broadcast_to(line, (count_x, 1, sz)), "gx", 0, 0)
    (adjoint,) = call(
        bind(finish_kernel, sx, sy), [(gradient.shape, F32)], parts, gradient, image_one, image_two
    )
    return adjoint


def solution(mesh):
    in_specs = (
        P(None, "gx", "gy", None),
        P(None, "gx", "gy", None),
        P(),
        P(),
        P(),
        P(None, "gx", "gy", None),
    )
    out_specs = P(None, "gx", "gy", None)
    return jax.shard_map(
        per_device, mesh=mesh, in_specs=in_specs, out_specs=out_specs, check_vma=False
    )
```

```python
import jax
import jax.numpy as jnp
from jax import lax
from jax.experimental import pallas as pl
from jax.experimental.pallas import tpu as pltpu
from jax.sharding import PartitionSpec as P


Q = 19
HID = 128
ITERS = 3
ROWS = 24
SHRINK = 16.0
FLOOR = 1e-10
VMEM_BYTES = 16 * 1024 * 1024
SPANS = (6, 6, 6)
FACE = 5

ORDER = (0, 4, 6, 8, 10, 2, 12, 14, 1, 5, 7, 9, 11, 3, 13, 15, 16, 17, 18)

F32 = jnp.float32
BF16 = jnp.bfloat16
VM = pl.BlockSpec(memory_space=pltpu.VMEM)
SM = pl.BlockSpec(memory_space=pltpu.SMEM)


def call(kernel, outs, *args):
    return pl.pallas_call(
        kernel,
        out_shape=[jax.ShapeDtypeStruct(shape, kind) for shape, kind in outs],
        in_specs=[SM if x.shape == (1,) else VM for x in args],
        out_specs=[VM] * len(outs),
        compiler_params=pltpu.CompilerParams(vmem_limit_bytes=VMEM_BYTES),
    )(*args)


def high(x):
    return x.astype(BF16).astype(F32)


def rows_dot(weights, x):
    top = high(x)
    stack = jnp.concatenate([top, top, x - top, jnp.zeros((8, x.shape[1]), F32)], axis=0)
    return jnp.dot(weights, stack.astype(BF16), preferred_element_type=F32)


def wide_dot(weights, x):
    top = x.astype(BF16)
    rest = (x - top.astype(F32)).astype(BF16)
    both = jnp.dot(weights, jnp.concatenate([top, rest], axis=0), preferred_element_type=F32)
    half = weights.shape[0] // 2
    return both[:half] + both[half:]


def together(chunks):
    chunks = list(chunks)
    for at in range(0, len(chunks), 4):
        running = chunks[at : at + 4]
        while running:
            running = [chunk for chunk in running if next(chunk, None)]


def weights_kernel(enter_t, middle, leave, enter_rows, leave_rows, middle_wide, middle_t_wide, enter_t_wide):
    def ordered(ref):
        rows = [ref[k : k + 1, :] for k in ORDER]
        return jnp.concatenate(rows + [jnp.zeros((ROWS - Q, HID), F32)], axis=0)

    def tall(rows):
        top = high(rows)
        stack = jnp.concatenate([top, rows - top, top, jnp.zeros((HID - 3 * ROWS, HID), F32)], axis=0)
        return stack.T.astype(BF16)

    def wide(mat):
        top = high(mat)
        rest = mat - top
        upper = jnp.concatenate([top, top], axis=1)
        lower = jnp.concatenate([rest, jnp.zeros_like(rest)], axis=1)
        return jnp.concatenate([upper, lower], axis=0).astype(BF16)

    enter = ordered(enter_t)
    enter_rows[...] = tall(enter)
    leave_rows[...] = tall(ordered(leave))
    middle_wide[...] = wide(middle[...])
    middle_t_wide[...] = wide(middle[...].T)
    scaled = enter * (1.0 / SHRINK)
    enter_t_wide[...] = wide(jnp.concatenate([scaled, jnp.zeros((8, HID), F32)], axis=0))


def offset_by(odd, low, high_):
    first = pl.multiple_of(jnp.where(odd, low, high_), 8)
    second = pl.multiple_of(jnp.where(odd, high_, low), 8)
    return first, second


def prepare_kernel(sx, sy, *refs):
    sources, odd, (field, state, to_first, to_second) = refs[:6], refs[6], refs[7:11]
    weights, (gradient, steady, links, sems) = refs[11:14], refs[14:]
    odd = odd[0] == 1
    copies = [
        pltpu.make_async_copy(source, target, sems.at[i])
        for i, (source, target) in enumerate(zip(sources, (gradient, steady, links, *weights)))
    ]
    for copy in copies:
        copy.start()
    blank = jnp.zeros((8, 128), F32)
    for x in range(sx):
        for y in range(sy):
            at = (x * sy + y) * ROWS + 16
            field[pl.ds(at, 8), :] = blank
            state[pl.ds(at, 8), :] = blank
    copies[0].wait()
    for x in range(sx):
        for row, k in enumerate(ORDER):
            field[pl.ds(x * sy * ROWS + row, sy, stride=ROWS), :] = gradient[k, x]
    copies[1].wait()
    copies[2].wait()
    for x in range(sx):
        for row, k in enumerate(ORDER):
            state[pl.ds(x * sy * ROWS + row, sy, stride=ROWS), :] = steady[k, x]
        for word in range(2):
            state[pl.ds(x * sy * ROWS + Q + word, sy, stride=ROWS), :] = links[word, x].astype(F32)
    at = 0
    for ref, depth in ((field, 3), (state, 2)):
        for x in range(sx):
            size = depth * ROWS
            first, second = offset_by(odd, x * sy * ROWS, (x * sy + sy - depth) * ROWS)
            to_first[pl.ds(at, size), :] = ref[pl.ds(first, size), :]
            to_second[pl.ds(at, size), :] = ref[pl.ds(second, size), :]
            at += size
    for copy in copies[3:]:
        copy.wait()


def sublane():
    return lax.broadcasted_iota(jnp.int32, (8, 128), 0)


def row_constants(values):
    row = sublane()
    out = jnp.zeros((8, 128), jnp.int32)
    for at, value in enumerate(values):
        out = jnp.where(row == at, value, out)
    return out


def codes_of(tail):
    word_0 = jnp.broadcast_to(tail[3:4, :].astype(jnp.int32), (8, 128))
    word_1 = jnp.broadcast_to(tail[4:5, :].astype(jnp.int32), (8, 128))
    solid = (word_1 & (1 << (18 - 10))) != 0
    codes = []
    for group in range(3):
        members = [ORDER[group * 8 + i] if group * 8 + i < Q else -1 for i in range(8)]
        second = row_constants([1 if k >= 10 else 0 for k in members])
        bit = row_constants([0 if k < 0 else 1 << (k % 10) for k in members])
        pad = row_constants([1 if k < 0 else 0 for k in members])
        word = jnp.where(second == 1, word_1, word_0)
        code = jnp.where((word & bit) != 0, 1.0, 0.0)
        codes.append(jnp.where(jnp.logical_or(solid, pad == 1), 2.0, code))
    return codes


def slopes_of(columns, enter_rows, middle_wide, slope_one, slope_two, codes):
    enter = enter_rows[:, 0:80]
    middle = middle_wide[...]

    def chunk(at):
        pair = [load() for load in columns[at : at + 2]]
        hidden = jnp.tanh(rows_dot(enter, jnp.concatenate(pair, axis=1)))
        yield True
        one = 1.0 - hidden * hidden
        hidden = jnp.tanh(wide_dot(middle, hidden))
        yield True
        two = 1.0 - hidden * hidden
        for i in range(2):
            slope_one[at + i] = one[:, i * 128 : (i + 1) * 128]
            slope_two[at + i] = two[:, i * 128 : (i + 1) * 128]
            for group, code in enumerate(codes_of(pair[i][16:24, :])):
                codes[at + i, group * 8 : group * 8 + 8, :] = code

    together(chunk(at) for at in range(0, len(columns), 2))


def loader(ref, offset):
    return lambda: ref[pl.ds(offset, ROWS), :]


def own_slopes_kernel(count, state, enter_rows, middle_wide, slope_one, slope_two, codes):
    columns = [loader(state, i * ROWS) for i in range(count)]
    slopes_of(columns, enter_rows, middle_wide, slope_one, slope_two, codes)


def halo_slopes_kernel(sx, low, high_, enter_rows, middle_wide, slope_one, slope_two, codes):
    columns = []
    for x in range(sx):
        for ref in (low, high_):
            for row in range(2):
                columns.append(loader(ref, (sx * 3 + x * 2 + row) * ROWS))
    slopes_of(columns, enter_rows, middle_wide, slope_one, slope_two, codes)


def side_slopes_kernel(sy, odd_x, first, second, enter_rows, middle_wide, slope_one, slope_two, codes):
    odd = jnp.full((ROWS, 128), odd_x[0]) == 1
    base = face_rows(sy + 6)

    def side(one, two, row):
        at = pl.ds(base + row * ROWS, ROWS)
        return lambda: jnp.where(odd, one[at, :], two[at, :])

    columns = [side(first, second, row) for row in range(sy + 2)]
    columns += [side(second, first, row) for row in range(sy + 2)]
    slopes_of(columns, enter_rows, middle_wide, slope_one, slope_two, codes)


def face_rows(height):
    return -(-(height * FACE + 8 - FACE) // 8) * 8


def face(out, base, at, rows):
    out[pl.ds(base + at * FACE, FACE), :] = rows[0:FACE]


def face_tail(base, height, *outs):
    used, size = height * FACE, face_rows(height)
    for out in outs:
        out[pl.ds(base + used, size - used), :] = jnp.zeros((size - used, out.shape[1]), F32)


def faces_kernel(sx, sy, odd_x, odd_y, field, state, first, second, _, low, high_, to_first, to_second):
    odd = jnp.full((8, 128), odd_y[0]) == 1
    for at in range(0, first.shape[0], 8):
        one, two = first[pl.ds(at, 8), :], second[pl.ds(at, 8), :]
        low[pl.ds(at, 8), :] = jnp.where(odd, one, two)
        high_[pl.ds(at, 8), :] = jnp.where(odd, two, one)
    face_tail(0, sy + 6, to_first, to_second)
    odd = jnp.full((8, 128), odd_x[0]) == 1
    for row in range(-3, sy + 3):
        down = column(sy, field, low, high_, 0, row, 0)
        up = column(sy, field, low, high_, sx - 1, row, 8)
        face(to_first, 0, row + 3, jnp.where(odd, down, up))
        face(to_second, 0, row + 3, jnp.where(odd, up, down))

    def state_column(x, row, group):
        if row < 0:
            return low[pl.ds((sx * 3 + x * 2 + row + 2) * ROWS + group, 8), :]
        if row >= sy:
            return high_[pl.ds((sx * 3 + x * 2 + row - sy) * ROWS + group, 8), :]
        return state[pl.ds((x * sy + row) * ROWS + group, 8), :]

    for row in range(-1, sy + 1):
        for group in (0, 8, 16):
            down, up = state_column(0, row, group), state_column(sx - 1, row, group)
            at = face_rows(sy + 6) + (row + 1) * ROWS + group
            to_first[pl.ds(at, 8), :] = jnp.where(odd, down, up)
            to_second[pl.ds(at, 8), :] = jnp.where(odd, up, down)


def column(sy, field, low, high_, x, row, group):
    if row < 0:
        return low[pl.ds((x * 3 + row + 3) * ROWS + group, 8), :]
    if row >= sy:
        return high_[pl.ds((x * 3 + row - sy) * ROWS + group, 8), :]
    return field[pl.ds((x * sy + row) * ROWS + group, 8), :]


def pull_column(get, code, x, row):
    at = sublane()
    straight = jnp.logical_or(at == 0, jnp.logical_or(at == 3, at == 4))
    first = jnp.logical_or(at == 3, at == 6)
    second = jnp.logical_or(at == 4, at == 7)
    own = [get(x, row, group) for group in (0, 8, 16)]
    out = []
    for group, step in ((0, 1), (8, -1)):
        value = jnp.where(straight, get(x + step, row, group), get(x, row + step, group))
        value = jnp.where(at == 1, get(x + step, row + step, group), value)
        value = jnp.where(at == 2, get(x + step, row - step, group), value)
        up = pltpu.roll(value, 127, 1)
        down = pltpu.roll(value, 1, 1)
        if step < 0:
            up, down = down, up
        out.append(jnp.where(first, up, jnp.where(second, down, value)))
    up = pltpu.roll(own[2], 127, 1)
    down = pltpu.roll(own[2], 1, 1)
    out.append(jnp.where(at == 0, up, jnp.where(at == 1, down, own[2])))
    swapped = jnp.where(at == 0, pltpu.roll(own[2], 7, 0), jnp.where(at == 1, pltpu.roll(own[2], 1, 0), own[2]))
    result = []
    for pulled, back, flag in zip(out, (own[1], own[0], swapped), (code(0), code(8), code(16))):
        result.append(jnp.where(flag == 0.0, pulled, jnp.where(flag == 1.0, back, 0.0)))
    return jnp.concatenate(result, axis=0)


def apply_rows(xs, first, last, get, table, weights, put, span):
    leave, middle, enter = weights[0][:, 0:80], weights[1][...], weights[2][...]

    def chunk(x, row):
        entries = [table(x, r) for r in range(row, min(row + span, last))]
        reads = [
            pull_column(get, lambda g, codes=codes, at=at: codes[at, g : g + 8, :], x, row + i)
            for i, (_, _, codes, at) in enumerate(entries)
        ]
        read = jnp.concatenate(reads, axis=1)
        yield True
        carried = rows_dot(leave, read) * jnp.concatenate([two[at] for _, two, _, at in entries], axis=1)
        yield True
        carried = wide_dot(middle, carried) * jnp.concatenate([one[at] for one, _, _, at in entries], axis=1)
        yield True
        image = (0.5 / SHRINK) * read + wide_dot(enter, carried)[:ROWS]
        for i in range(len(entries)):
            put(x, row + i, image[:, i * 128 : (i + 1) * 128])

    together(chunk(x, row) for x in xs for row in range(first, last, span))


def table_of(sx, sy, refs, side=None):
    one, two, codes, one_h, two_h, codes_h = refs

    def table(x, row):
        if not 0 <= x < sx:
            return *side, (row + 1 if x < 0 else sy + 2 + row + 1)
        if 0 <= row < sy:
            return one, two, codes, x * sy + row
        return one_h, two_h, codes_h, x * 4 + (row + 2 if row < 0 else row - sy + 2)

    return table


def sorted_loads(odd, first, second):
    seen = {}

    def get(at):
        if at not in seen:
            one, two = first[pl.ds(at, 8), :], second[pl.ds(at, 8), :]
            seen[at] = jnp.where(odd, one, two), jnp.where(odd, two, one)
        return seen[at]

    return get


def first_kernel(sx, sy, odd_x, field, low, high_, first, second, *refs):
    tables, weights, (image, to_first, to_second) = refs[:6], refs[6:9], refs[9:]
    beside = sorted_loads(jnp.full((8, 128), odd_x[0]) == 1, first, second)
    height = sy + 4

    def get(x, row, group):
        if x < 0:
            return beside((row + 3) * FACE)[0]
        if x >= sx:
            return beside((row + 3) * FACE)[1]
        return column(sy, field, low, high_, x, row, group)

    def put(x, row, value):
        image[pl.ds((x * height + row + 2) * ROWS, ROWS), :] = value

    near = height * ROWS
    apply_rows(range(sx), -2, sy + 2, get, table_of(sx, sy, tables), weights, put, SPANS[0])
    odd = odd_x[0] == 1
    columns = offset_by(odd, 0, (sx - 1) * near)
    faces = offset_by(odd, near, (sx - 2) * near + 8)
    for out, at, face_at in zip((to_first, to_second), columns, faces):
        for row in range(height):
            here = row * ROWS
            out[pl.ds(here, 16), :] = image[pl.ds(at + here, 16), :]
            crossing = pltpu.roll(image[pl.ds(face_at + here, 8), :], Q - 16, 0)
            out[pl.ds(here + 16, 8), :] = jnp.where(sublane() < Q - 16, image[pl.ds(at + here + 16, 8), :], crossing)


def second_kernel(sx, sy, odd_x, previous, first, second, *refs):
    tables, side, weights, image = refs[:6], refs[6:9], refs[9:12], refs[12]
    beside = sorted_loads(jnp.full((8, 128), odd_x[0]) == 1, first, second)
    height = sy + 4

    def get(x, row, group):
        if 0 <= x < sx:
            return previous[pl.ds((x * height + row + 2) * ROWS + group, 8), :]
        if x in (-1, sx):
            return beside((row + 2) * ROWS + group)[0 if x < 0 else 1]
        return pltpu.roll(beside((row + 2) * ROWS + 16)[0 if x < 0 else 1], 24 - Q, 0)

    def put(x, row, value):
        image[pl.ds(((x + 1) * (sy + 2) + row + 1) * ROWS, ROWS), :] = value

    apply_rows(range(-1, sx + 1), -1, sy + 1, get, table_of(sx, sy, tables, side), weights, put, SPANS[1])


def third_kernel(sx, sy, previous, *refs):
    tables, weights, (field, image_one, out) = refs[:6], refs[6:9], refs[9:]

    def get(x, row, group):
        return previous[pl.ds(((x + 1) * (sy + 2) + row + 1) * ROWS + group, 8), :]

    totals = [jnp.zeros((8, 128), F32) for _ in range(10)]

    def put(x, row, value):
        for group in (0, 8, 16):
            parts = (
                field[pl.ds((x * sy + row) * ROWS + group, 8), :],
                image_one[pl.ds((x * (sy + 4) + row + 2) * ROWS + group, 8), :],
                get(x, row, group),
                value[group : group + 8],
            )
            at = 0
            for i in range(4):
                for j in range(i, 4):
                    totals[at] = totals[at] + parts[i] * parts[j]
                    at += 1

    apply_rows(range(sx), 0, sy, get, table_of(sx, sy, tables), weights, put, SPANS[2])
    sums = jnp.concatenate(
        [jnp.sum(total, axis=0, keepdims=True) for total in totals] + [jnp.zeros((6, 128), F32)], axis=0
    )
    sums = jnp.broadcast_to(jnp.sum(sums, axis=1, keepdims=True), (16, 128))
    place = lax.broadcasted_iota(jnp.int32, (16, 128), 0) == lax.broadcasted_iota(jnp.int32, (16, 128), 1)
    line = jnp.sum(jnp.where(place, sums, 0.0), axis=0, keepdims=True)
    for i in range(out.shape[0]):
        out[i] = line


def least_squares(hess, target):
    rows = [list(line) for line in hess]
    target = list(target)
    for col in range(ITERS):
        upper = rows[col][col]
        lower = rows[col + 1][col]
        radius = jnp.sqrt(upper * upper + lower * lower)
        cosine = upper / radius
        sine = lower / radius
        for other in range(col, ITERS):
            first_value = rows[col][other]
            second_value = rows[col + 1][other]
            rows[col][other] = cosine * first_value + sine * second_value
            rows[col + 1][other] = cosine * second_value - sine * first_value
        first_value = target[col]
        second_value = target[col + 1]
        target[col] = cosine * first_value + sine * second_value
        target[col + 1] = cosine * second_value - sine * first_value
    coeffs = [None] * ITERS
    for col in reversed(range(ITERS)):
        accum = target[col]
        for other in range(col + 1, ITERS):
            accum = accum - rows[col][other] * coeffs[other]
        coeffs[col] = accum / rows[col][col]
    return coeffs


def finish_kernel(sx, sy, parts, gradient, image_one, image_two, out):
    total = parts[0]
    for i in range(1, parts.shape[0]):
        total = total + parts[i]
    total = jnp.broadcast_to(total, (8, 128))
    lane = lax.broadcasted_iota(jnp.int32, (8, 128), 1)
    gram = [[None] * 4 for _ in range(4)]
    at = 0
    for i in range(4):
        for j in range(i, 4):
            one = jnp.sum(jnp.where(lane == at, total, 0.0), axis=1, keepdims=True)
            gram[i][j] = gram[j][i] = jnp.broadcast_to(one, (8, 128))
            at += 1
    size = [jnp.sqrt(gram[i][i]) for i in range(4)]
    inverse = [1.0 / value for value in size]
    cosines = [[gram[i][j] * inverse[i] * inverse[j] for j in range(4)] for i in range(4)]
    zero = jnp.zeros((8, 128), F32)
    one = zero + 1.0
    lower = [[zero] * 4 for _ in range(4)]
    for i in range(4):
        for j in range(i + 1):
            value = one if i == j else cosines[i][j]
            for k in range(j):
                value = value - lower[i][k] * lower[j][k]
            lower[i][j] = jnp.sqrt(jnp.maximum(value, FLOOR)) if i == j else value / lower[j][j]
    hess = [[zero] * ITERS for _ in range(ITERS + 1)]
    for j in range(ITERS):
        ratio = SHRINK * size[j + 1] * inverse[j]
        for i in range(j + 2):
            hess[i][j] = lower[j][i] - ratio * lower[j + 1][i]
    coeffs = least_squares(hess, [one, zero, zero, zero])
    scaled = [coeffs[j] * size[0] * inverse[j] for j in range(ITERS)]
    for x in range(sx):
        for row, k in enumerate(ORDER):
            second = image_one[pl.ds((x * (sy + 4) + 2) * ROWS + row, sy, stride=ROWS), :]
            third = image_two[pl.ds(((x + 1) * (sy + 2) + 1) * ROWS + row, sy, stride=ROWS), :]
            out[k, x] = scaled[0] * gradient[k, x] + scaled[1] * second + scaled[2] * third


def exchange(axis, to_first, to_second):
    count = lax.axis_size(axis)
    near = [(i, i ^ 1) for i in range(count)]
    far = [(i, ((i + 1) ^ 1) - 1) for i in range(1, count - 1)]
    second = lax.ppermute(to_second, axis, far)
    first = lax.ppermute(to_first, axis, near)
    return first, second


def per_device(gradient, steady_state, enter_weight, middle_weight, leave_weight, links):
    sx, sy, sz = gradient.shape[1:]
    own = sx * sy
    odd_x, odd_y = [(lax.axis_index(axis) % 2).reshape(1) for axis in ("gx", "gy")]

    def bind(kernel, *static):
        def bound(*refs):
            kernel(*static, *refs)

        bound.__name__ = kernel.__name__
        return bound

    flat = (own * ROWS, sz)
    message = (sx * 5 * ROWS, sz)
    fetched = (gradient, steady_state, links, enter_weight.T, middle_weight, leave_weight)
    field, state, to_first, to_second, *fetched_weights = pl.pallas_call(
        bind(prepare_kernel, sx, sy),
        out_shape=[jax.ShapeDtypeStruct(shape, F32) for shape in (flat, flat, message, message)]
        + [jax.ShapeDtypeStruct(x.shape, x.dtype) for x in fetched[3:]],
        in_specs=[pl.BlockSpec(memory_space=pltpu.HBM)] * 6 + [SM],
        out_specs=[VM] * 7,
        scratch_shapes=[pltpu.VMEM(x.shape, x.dtype) for x in (gradient, steady_state, links)]
        + [pltpu.SemaphoreType.DMA((6,))],
        compiler_params=pltpu.CompilerParams(vmem_limit_bytes=VMEM_BYTES),
    )(*[pltpu.with_memory_space_constraint(x, pltpu.HBM) for x in fetched], odd_y)
    first, second = exchange("gy", to_first, to_second)
    enter_rows, leave_rows, middle_wide, middle_t_wide, enter_t_wide = call(
        weights_kernel,
        [((HID, HID), BF16), ((HID, HID), BF16), ((2 * HID, 2 * HID), BF16), ((2 * HID, 2 * HID), BF16), ((64, 2 * HID), BF16)],
        *fetched_weights,
    )

    def tables(count):
        return [((count, HID, sz), F32), ((count, HID, sz), F32), ((count, ROWS, sz), F32)]

    own_table = call(bind(own_slopes_kernel, own), tables(own), state, enter_rows, middle_wide)
    low, high_, to_first, to_second = call(
        bind(faces_kernel, sx, sy),
        [(message, F32)] * 2 + [((face_rows(sy + 6) + (sy + 2) * ROWS, sz), F32)] * 2,
        odd_x, odd_y, field, state, first, second, own_table[2],
    )
    first, second = exchange("gx", to_first, to_second)
    halo_table = call(
        bind(halo_slopes_kernel, sx), tables(sx * 4), low, high_, enter_rows, middle_wide
    )
    tables_here, weights = (*own_table, *halo_table), (leave_rows, middle_t_wide, enter_t_wide)
    height = sy + 4
    side_message = (height * ROWS, sz)
    image_one, to_first, to_second = call(
        bind(first_kernel, sx, sy),
        [((sx * height * ROWS, sz), F32), (side_message, F32), (side_message, F32)],
        odd_x, field, low, high_, first, second, *tables_here, *weights,
    )
    side_table = call(
        bind(side_slopes_kernel, sy), tables(2 * (sy + 2)), odd_x, first, second, enter_rows, middle_wide
    )
    first, second = exchange("gx", to_first, to_second)
    (image_two,) = call(
        bind(second_kernel, sx, sy),
        [(((sx + 2) * (sy + 2) * ROWS, sz), F32)],
        odd_x, image_one, first, second, *tables_here, *side_table, *weights,
    )
    count_y = lax.axis_size("gy")
    count_x = lax.axis_size("gx")

    (line,) = call(
        bind(third_kernel, sx, sy),
        [((count_y, 1, sz), F32)],
        image_two, *tables_here, *weights, field, image_one,
    )
    line = jnp.sum(lax.all_to_all(line, "gy", 0, 0), axis=0, keepdims=True)
    parts = lax.all_to_all(jnp.broadcast_to(line, (count_x, 1, sz)), "gx", 0, 0)
    (adjoint,) = call(
        bind(finish_kernel, sx, sy), [(gradient.shape, F32)], parts, gradient, image_one, image_two
    )
    return adjoint


def solution(mesh):
    in_specs = (
        P(None, "gx", "gy", None),
        P(None, "gx", "gy", None),
        P(),
        P(),
        P(),
        P(None, "gx", "gy", None),
    )
    out_specs = P(None, "gx", "gy", None)
    return jax.shard_map(
        per_device, mesh=mesh, in_specs=in_specs, out_specs=out_specs, check_vma=False
    )
```
